256 devices in a mesh: dp: 4 (over x_lo, core), seq: 64 (over x_hi, z, y).
Axes of the slice: x: 4 (x_hi: 2, x_lo: 2; x = x_hi * 2 + x_lo), y: 4, z: 8, core: 2. Of those that a mesh axis runs over, the one named last changes fastest.
Arguments:
- hidden: bfloat16 [4, 8192, 2048], P('dp', 'seq'), may hold values from -16 to 16
- tokens: int32 [4, 8192], P('dp', 'seq'), may hold values from 0 to 4
- embedding: float32 [5, 2048], replicated, may hold values from -6 to 6
- weight: bfloat16 [2048, 1024], P('dp'), may hold values from -0.125 to 0.125
- kernel: float32 [7, 1024], replicated, may hold values from -2.4 to 2.4
- cotangent: bfloat16 [4, 8192, 1024], P('dp', 'seq'), may hold values from -6 to 6
Outputs:
- block_result: bfloat16 [4, 8192, 1024], P('dp', 'seq')
- grad_hidden: bfloat16 [4, 8192, 2048], P('dp', 'seq')
- grad_weight: float32 [2048, 1024], P('dp')
- grad_kernel: float32 [7, 1024], replicated
- grad_embedding: float32 [5, 2048], replicated
The draws below stay inside these ranges and needn't reach their ends.
All inputs are finite; a program needn't handle non-finite values.
Results may differ from the reference program's by a relative error of at most 0.0095.
Values may be sent and summed in bfloat16 or wider, within the bound.
No kernel may reach another device: no remote copies, remote signals or barrier semaphores. Data moves between devices by JAX's collectives and lax.ppermute only.
A program may use at most 64 MiB of HBM per device.

```python
import math
import jax
import jax.numpy as jnp
from jax import lax

D = 2048
UNITS = 1024
VOCAB = 5
REACH = 3
TAPS = 7
LENGTH = 8192
BATCH = 4


def place_ends(drawn, rng, smallest, high):
    dims = drawn.shape
    place = [jax.random.randint(jax.random.fold_in(rng, axis), (), 0, dims[axis]) for axis in range(len(dims))]
    drawn = drawn.at[tuple(place)].set(smallest)
    longest = dims.index(max(dims))
    place[longest] = (place[longest] + 1) % dims[longest]
    return drawn.at[tuple(place)].set(high)


def raised(array, own_key, source, target, shards_of, factor):
    owner, partner = [(jnp.arange(array.shape[axis_at]) // (array.shape[axis_at] // shards_of)).reshape([-1 if axis == axis_at else 1 for axis in range(array.ndim)]) for axis_at in (source, target)]
    chosen = jax.random.permutation(own_key, shards_of)[partner]
    strong = (owner == chosen) | (owner == (partner + shards_of // 2) % shards_of)
    return jnp.where(strong, factor * array, array)


def block_levels(stream_key, dims, split, least, largest):
    loudness = 1.0
    for position, shards_of in split:
        steps = jax.random.uniform(jax.random.fold_in(jax.random.fold_in(stream_key, 6), position), (shards_of,), jnp.float32, least / len(split), largest / len(split))
        loudness = loudness * jnp.repeat(jnp.exp(steps), dims[position] // shards_of).reshape((-1,) + (1,) * (len(dims) - 1 - position))
    return loudness


def normal_values(own_key, dims, deviation, reach, cuts=(), kind=jnp.bfloat16):
    entries = jax.random.normal(own_key, dims, jnp.float32) * deviation
    if len(cuts) > 0:
        entries = block_levels(own_key, dims, cuts, -0.22, 0.18) * entries
    return jnp.clip(entries, min=-reach, max=reach).astype(kind)


def noise_with(key, shape, spread, limit, shards, heavy, held_as=jnp.bfloat16):
    result = spread * jax.random.normal(key, shape, jnp.float32)
    if shards:
        result = result * block_levels(key, shape, shards, -0.22, 0.18)
    return jnp.clip(raised(result, jax.random.fold_in(key, 3), *heavy), -limit, limit).astype(held_as)


def setup_inputs(seed: int = 0) -> dict:
    seeds = jax.random.split(jax.random.key(seed), 7)
    return {
        "hidden": noise_with(seeds[0], (BATCH, LENGTH, D), 1.0, 16.0, ((0, 4), (1, 64)), (1, 2, 64, 4.0)),
        "tokens": place_ends(jax.random.randint(seeds[1], (BATCH, LENGTH), 0, VOCAB), jax.random.fold_in(seeds[1], 1), 0, VOCAB - 1).astype(jnp.int32),
        "embedding": normal_values(seeds[2], (VOCAB, D), 1.0, 6.0, (), jnp.float32),
        "weight": normal_values(seeds[3], (D, UNITS), D ** -0.5, 0.125, ((0, 4),)),
        "kernel": normal_values(seeds[4], (TAPS, UNITS), 0.4, 2.4, (), jnp.float32),
        "cotangent": normal_values(seeds[5], (BATCH, LENGTH, UNITS), 1.0, 6.0, ((0, 4), (1, 64))),
    }


def lookup(token_codes, embedding):
    running = jnp.zeros((token_codes.shape[0], embedding.shape[1]), jnp.float32)
    for symbol in range(embedding.shape[0]):
        running = running + jnp.where((token_codes == symbol)[:, None], embedding[symbol][None, :], 0.0)
    return running

def strand(inputs, upstream, weight, kernel):
    values = jnp.dot(inputs, weight, preferred_element_type=jnp.float32).astype(jnp.bfloat16)
    linear = values.astype(jnp.float32)
    widened = jnp.pad(linear, ((REACH, REACH), (0, 0)))
    mixing = kernel[0][None, :] * widened[0:LENGTH]
    for tap_index in range(1, TAPS):
        mixing = mixing + kernel[tap_index][None, :] * widened[tap_index:tap_index + LENGTH]
    logistic = jax.nn.sigmoid(linear)
    gating = linear * logistic
    strand_out = mixing * gating
    incoming = upstream.astype(jnp.float32)
    grad_mix = incoming * gating
    accumulated = incoming * mixing * logistic * (1.0 + linear * (1.0 - logistic))
    grad_padded = jnp.pad(grad_mix, ((REACH, REACH), (0, 0)))
    for tap_index in range(TAPS):
        lower = 2 * REACH - tap_index
        accumulated = accumulated + kernel[tap_index][None, :] * grad_padded[lower:lower + LENGTH]
    grad_values = accumulated.astype(jnp.bfloat16)
    kernel_grad = jnp.stack([lax.optimization_barrier(jnp.sum(grad_mix * widened[tap_index:tap_index + LENGTH], axis=0)) for tap_index in range(TAPS)])
    weight_grad = jnp.dot(inputs.T, grad_values, preferred_element_type=jnp.float32)
    returned = jnp.dot(grad_values, weight.T, preferred_element_type=jnp.float32)
    return (strand_out, kernel_grad, weight_grad, returned)

def one_window(window, token_codes, upstream, embedding, weight, kernel):
    stream = (window.astype(jnp.float32) + lookup(token_codes, embedding)).astype(jnp.bfloat16)
    reverse = stream[::-1, ::-1]
    out_fwd, kernel_fwd, weight_fwd, back_fwd = strand(stream, upstream, weight, kernel)
    out_rev, kernel_rev, weight_rev, back_rev = strand(reverse, upstream[::-1, ::-1], weight, kernel)
    rev_out = out_rev.astype(jnp.bfloat16)
    block_result = (out_fwd + rev_out.astype(jnp.float32)[::-1, ::-1]).astype(jnp.bfloat16)
    back_round = back_rev.astype(jnp.bfloat16)
    grad_stream = back_fwd + back_round.astype(jnp.float32)[::-1, ::-1]
    one_hot = (token_codes[:, None] == jnp.arange(VOCAB, dtype=jnp.int32)[None, :]).astype(jnp.float32)
    table_part = lax.dot_general(one_hot, grad_stream, (((0,), (0,)), ((), ())), precision=lax.Precision.HIGHEST, preferred_element_type=jnp.float32)
    return (block_result, grad_stream.astype(jnp.bfloat16), weight_fwd + weight_rev, kernel_fwd + kernel_rev, table_part)

def reference(hidden, tokens, embedding, weight, kernel, cotangent):
    block_result, grad_hidden, weight_all, kernel_all, table_all = lax.map(lambda pieces: one_window(pieces[0], pieces[1], pieces[2], embedding, weight, kernel), (hidden, tokens, cotangent))
    factor = 1.0 / math.sqrt(BATCH * LENGTH)
    return (block_result, grad_hidden, lax.optimization_barrier(jnp.sum(weight_all, axis=0)) * factor, lax.optimization_barrier(jnp.sum(kernel_all, axis=0)) * factor, lax.optimization_barrier(jnp.sum(table_all, axis=0)) * factor)
```

```python
import math

import jax
import jax.numpy as jnp
import numpy as np
from jax import lax
from jax.sharding import Mesh, PartitionSpec as P

AXES = ("xl", "c", "xh", "z", "y")
SIZES = (2, 2, 2, 8, 4)
EDGE = 8


def shift(cells, axes, target):
    sizes = [SIZES[AXES.index(axis)] for axis in axes]
    pairs = []
    for place in np.ndindex(*sizes):
        goal = target(*place)
        if goal is not None:
            pairs.append((int(np.ravel_multi_index(place, sizes)), int(np.ravel_multi_index(goal, sizes))))
    return lax.ppermute(cells, axes if len(axes) > 1 else axes[0], pairs)


def swap_core(cells):
    return shift(cells, ("c",), lambda c: (1 - c,))


def side_x(xl, c, xh):
    x = (2 * xh + xl + (1 if c == 0 else 3)) % 4
    return (x % 2, c, x // 2)


def turn_x(xl, xh):
    x = 3 - (2 * xh + xl)
    return (x % 2, x // 2)


def neighbour(step):
    def target(xh, z, y):
        place = (xh * 8 + z) * 4 + y + step
        if not 0 <= place < 64:
            return None
        return (place // 32, place // 4 % 8, place % 4)

    return target


def sum_everywhere(cells):
    cells = cells + swap_core(cells)
    cells = cells + shift(cells, ("xl",), lambda a: (1 - a,))
    cells = cells + shift(cells, ("xl", "xh"), turn_x)
    cells = cells + shift(cells, ("y",), lambda a: (a ^ 1,))
    cells = cells + shift(cells, ("y",), lambda a: (3 - a,))
    cells = cells + shift(cells, ("z",), lambda a: (a ^ 1,))
    cells = cells + shift(cells, ("z",), lambda a: (a ^ 2,))
    return cells + shift(cells, ("z",), lambda a: (7 - a,))


def added(*parts):
    total = parts[0].astype(jnp.float32)
    for part in parts[1:]:
        total = total + part.astype(jnp.float32)
    return total


def reduce_rows(own, mate, side, side_mate):
    side_sum = added(side, swap_core(side_mate)).astype(jnp.bfloat16)
    from_side = shift(side_sum, ("xl", "c", "xh"), side_x)
    block = added(own, swap_core(mate), from_side).astype(jnp.bfloat16)
    y = lax.axis_index("y")
    rows = block.shape[0] // 4
    parts = [lax.dynamic_slice_in_dim(block, y * rows, rows, 0)]
    for step in (1, 2, 3):
        chunk = lax.dynamic_slice_in_dim(block, (y + step) % 4 * rows, rows, 0)
        parts.append(shift(chunk, ("y",), lambda a: ((a + step) % 4,)))
    quarter = added(*parts).astype(jnp.bfloat16)
    pieces = quarter.reshape(16, rows // 16, -1)
    pieces = lax.all_to_all(pieces, ("xh", "z"), split_axis=0, concat_axis=0, tiled=True)
    piece = jnp.sum(pieces.astype(jnp.float32), axis=0).astype(jnp.bfloat16)
    pieces = lax.all_to_all(
        jnp.broadcast_to(piece[None], pieces.shape), ("xh", "z"), split_axis=0, concat_axis=0, tiled=True
    )
    quarter = pieces.reshape(rows, -1)
    quarters = [quarter] + [shift(quarter, ("y",), lambda a: ((a + step) % 4,)) for step in (1, 2, 3)]
    stacked = jnp.stack(quarters)
    return jnp.concatenate([stacked[(y - row) % 4] for row in range(4)], axis=0)


def local(hidden, tokens, embedding, weight, kernel, cotangent):
    window = hidden[0]
    token_codes = tokens[0]
    upstream = cotangent[0]
    rows, features = window.shape
    units = weight.shape[1]
    taps = kernel.shape[0]
    reach = (taps - 1) // 2
    factor = 1.0 / math.sqrt(rows * 256)
    width = features // 4
    me = 2 * lax.axis_index("xl") + lax.axis_index("c")
    blocks = [me ^ r for r in range(4)]
    weights = [weight, swap_core(weight), shift(weight, ("xl", "c", "xh"), side_x)]
    weights.append(swap_core(weights[2]))

    looked = jnp.zeros((rows, features), jnp.float32)
    for symbol in range(embedding.shape[0]):
        looked = looked + jnp.where((token_codes == symbol)[:, None], embedding[symbol][None, :], 0.0)
    stream = (window.astype(jnp.float32) + looked).astype(jnp.bfloat16)
    both = jnp.concatenate([stream, upstream], axis=1)
    before = shift(both[rows - EDGE :], ("xh", "z", "y"), neighbour(1))
    after = shift(both[:EDGE], ("xh", "z", "y"), neighbour(-1))
    wide = jnp.concatenate([before, both, after], axis=0)
    total = rows + 2 * EDGE

    def exchange(size):
        return (
            lax.broadcasted_iota(jnp.int32, (size, size), 0) + lax.broadcasted_iota(jnp.int32, (size, size), 1)
            == size - 1
        ).astype(jnp.bfloat16)

    def flipped(cells):
        size = 256
        count = cells.shape[1] // size
        turn = exchange(size)
        return jnp.concatenate(
            [
                jnp.dot(
                    cells[:, (count - 1 - at) * size : (count - at) * size],
                    turn,
                    preferred_element_type=jnp.float32,
                ).astype(jnp.bfloat16)
                for at in range(count)
            ],
            axis=1,
        )

    forward = [lax.dynamic_slice_in_dim(wide, at * width, width, 1) for at in blocks]
    reverse = [flipped(forward[r ^ 3]) for r in range(4)]
    stacks = [jnp.concatenate([forward[r], reverse[r]], axis=0) for r in range(4)]
    projected = sum(jnp.dot(stacks[r], weights[r], preferred_element_type=jnp.float32) for r in range(4))
    values = projected.astype(jnp.bfloat16).astype(jnp.float32)
    values = [values[:total], values[total:]]
    ups = wide[:, features:]
    ups = [ups.astype(jnp.float32), flipped(ups).astype(jnp.float32)]
    outs = []
    grads = []
    kernel_part = jnp.zeros((taps, units), jnp.float32)
    for way in range(2):
        offsets = [EDGE + (tap - reach if way == 0 else reach - tap) for tap in range(taps)]
        linear = values[way]
        logistic = jax.nn.sigmoid(linear)
        gating = linear * logistic
        grad_mix = ups[way] * gating
        mixing = kernel[0][None] * linear[offsets[0] : offsets[0] + rows]
        for tap in range(1, taps):
            mixing = mixing + kernel[tap][None] * linear[offsets[tap] : offsets[tap] + rows]
        mid = slice(EDGE, EDGE + rows)
        outs.append(mixing * gating[mid])
        accumulated = ups[way][mid] * mixing * logistic[mid] * (1.0 + linear[mid] * (1.0 - logistic[mid]))
        for tap in range(taps):
            lower = 2 * EDGE - offsets[tap]
            accumulated = accumulated + kernel[tap][None] * grad_mix[lower : lower + rows]
        grads.append(accumulated.astype(jnp.bfloat16))
        kernel_part = kernel_part + jnp.stack(
            [jnp.sum(grad_mix[mid] * linear[at : at + rows], axis=0) for at in offsets]
        )
    block_result = (outs[0] + flipped(outs[1].astype(jnp.bfloat16)).astype(jnp.float32)).astype(jnp.bfloat16)
    grad_stack = jnp.concatenate(grads, axis=0)
    mids = [jnp.concatenate([forward[r][EDGE : EDGE + rows], reverse[r][EDGE : EDGE + rows]], axis=0) for r in range(4)]
    products = [
        lax.dot_general(
            mids[r], grad_stack, (((0,), (0,)), ((), ())), preferred_element_type=jnp.float32
        ).astype(jnp.bfloat16)
        for r in range(4)
    ]
    grad_weight = reduce_rows(*products).astype(jnp.float32) * factor
    backs = [
        lax.dot_general(grad_stack, weights[r], (((1,), (1,)), ((), ())), preferred_element_type=jnp.float32)
        for r in range(4)
    ]
    streams = jnp.stack(
        [backs[r][:rows] + flipped(backs[r ^ 3][rows:].astype(jnp.bfloat16)).astype(jnp.float32) for r in range(4)]
    )
    grad_stream = jnp.concatenate([streams[at ^ me] for at in range(4)], axis=1)
    one_hot = (jnp.arange(embedding.shape[0], dtype=jnp.int32)[:, None] == token_codes[None, :]).astype(jnp.float32)
    table_part = jnp.dot(one_hot, grad_stream, precision=lax.Precision.HIGHEST, preferred_element_type=jnp.float32)
    small = jnp.concatenate([kernel_part, table_part.reshape(-1, units)], axis=0)
    small = sum_everywhere(small) * factor
    return (
        block_result[None],
        grad_stream.astype(jnp.bfloat16)[None],
        grad_weight,
        small[:taps],
        small[taps:].reshape(embedding.shape),
    )


def solution(mesh):
    fine = Mesh(mesh.devices.reshape(SIZES), AXES)
    batch = ("xl", "c")
    place = ("xh", "z", "y")
    in_specs = (P(batch, place, None), P(batch, place), P(), P(batch, None), P(), P(batch, place, None))
    out_specs = (P(batch, place, None), P(batch, place, None), P(batch, None), P(), P())
    return jax.shard_map(local, mesh=fine, in_specs=in_specs, out_specs=out_specs, check_vma=False)
```

```python
import functools
import math

import jax
import jax.numpy as jnp
import numpy as np
from jax import lax
from jax.experimental import pallas as pl
from jax.experimental.pallas import tpu as pltpu
from jax.sharding import Mesh, PartitionSpec as P

AXES = ("xl", "c", "xh", "z", "y")
SIZES = (2, 2, 2, 8, 4)
EDGE = 8
REACH = 3
TAPS = 7
LANES = 128
PACK = 32


def shift(cells, axes, target):
    sizes = [SIZES[AXES.index(axis)] for axis in axes]
    pairs = []
    for place in np.ndindex(*sizes):
        goal = target(*place)
        if goal is not None:
            pairs.append((int(np.ravel_multi_index(place, sizes)), int(np.ravel_multi_index(goal, sizes))))
    return lax.ppermute(cells, axes if len(axes) > 1 else axes[0], pairs)


def swap_core(cells):
    return shift(cells, ("c",), lambda c: (1 - c,))


def side_x(xl, c, xh):
    x = (2 * xh + xl + (1 if c == 0 else 3)) % 4
    return (x % 2, c, x // 2)


def turn_x(xl, xh):
    x = 3 - (2 * xh + xl)
    return (x % 2, x // 2)


def neighbour(step):
    def target(xh, z, y):
        place = (xh * 8 + z) * 4 + y + step
        if not 0 <= place < 64:
            return None
        return (place // 32, place // 4 % 8, place % 4)

    return target


def added(*parts):
    total = parts[0].astype(jnp.float32)
    for part in parts[1:]:
        total = total + part.astype(jnp.float32)
    return total


def low_lanes(shape):
    return lax.broadcasted_iota(jnp.int32, shape, len(shape) - 1) < LANES // 2


def paired(cells):
    whole = cells + pltpu.roll(cells, LANES // 2, 1)
    head = whole.astype(jnp.bfloat16).astype(jnp.float32)
    return jnp.where(low_lanes(cells.shape), head, whole - head)


def thirds(cells):
    head = cells.astype(jnp.bfloat16)
    rest = cells - head.astype(jnp.float32)
    middle = rest.astype(jnp.bfloat16)
    return jnp.concatenate([head, middle, (rest - middle.astype(jnp.float32)).astype(jnp.bfloat16)], axis=0)


def turning(size):
    place = lax.broadcasted_iota(jnp.int32, (size, size), 0) + lax.broadcasted_iota(jnp.int32, (size, size), 1)
    return (place == size - 1).astype(jnp.bfloat16)


def strand_kernel(stacks, w0, w1, w2, w3, ups, taps, hot, out, grads, extra, values, mixes, sums):
    total = stacks.shape[1] // 2
    rows = total - 2 * EDGE
    units = w0.shape[1]
    count = units // LANES

    def project(at, _):
        cols = pl.ds(pl.multiple_of(at * 256, 256), 256)
        acc = jnp.zeros((2 * total, 256), jnp.float32)
        for r, w in enumerate((w0, w1, w2, w3)):
            acc = acc + jnp.dot(stacks[r], w[:, cols], preferred_element_type=jnp.float32)
        values[:, cols] = acc.astype(jnp.bfloat16).astype(jnp.float32)
        return 0

    lax.fori_loop(0, units // 256, project, 0)
    sums[...] = jnp.zeros(sums.shape, jnp.float32)
    turn = turning(LANES)

    def work(at, _):
        outs = []
        for way in range(2):
            block = at if way == 0 else count - 1 - at
            cols = pl.ds(pl.multiple_of(block * LANES, LANES), LANES)
            base = way * total
            places = [base + EDGE + (tap - REACH if way == 0 else REACH - tap) for tap in range(TAPS)]
            linear = values[base : base + total, cols]
            logistic = jax.nn.sigmoid(linear)
            gating = linear * logistic
            up = ups[base : base + total, cols].astype(jnp.float32)
            grad_mix = up * gating
            mixes[way] = grad_mix
            mid = slice(EDGE, EDGE + rows)
            linear, logistic, gating, up, grad_mix = [
                cells[mid] for cells in (linear, logistic, gating, up, grad_mix)
            ]
            mixing = jnp.zeros((rows, LANES), jnp.float32)
            for tap in range(TAPS):
                moved = values[places[tap] : places[tap] + rows, cols]
                mixing = mixing + taps[tap : tap + 1, cols] * moved
                sums[tap : tap + 1, cols] += jnp.sum(grad_mix * moved, axis=0, keepdims=True)
            outs.append(mixing * gating)
            acc = up * mixing * logistic * (1.0 + linear * (1.0 - logistic))
            for tap in range(TAPS):
                lower = 2 * EDGE - places[tap] + base
                acc = acc + taps[tap : tap + 1, cols] * mixes[way, lower : lower + rows]
            grads[way * rows : (way + 1) * rows, cols] = acc.astype(jnp.bfloat16)
        turned = jnp.dot(outs[1].astype(jnp.bfloat16), turn, preferred_element_type=jnp.float32)
        out[:, pl.ds(pl.multiple_of(at * LANES, LANES), LANES)] = (outs[0] + turned).astype(jnp.bfloat16)
        return 0

    lax.fori_loop(0, count, work, 0)
    by_token = [
        jnp.dot(hot[...], grads[way * rows : (way + 1) * rows], preferred_element_type=jnp.float32)
        for way in range(2)
    ]
    for at in range(count):
        cols = slice(at * LANES, (at + 1) * LANES)
        pack = jnp.concatenate(
            [sums[:, cols], by_token[0][:8, cols], by_token[1][:8, cols], jnp.zeros((8, LANES), jnp.float32)], axis=0
        )
        head = pack.astype(jnp.bfloat16).astype(jnp.float32)
        rest = pack - head
        low = low_lanes(pack.shape)
        first = jnp.where(low, head, pltpu.roll(rest, LANES // 2, 1))
        second = jnp.where(low, pltpu.roll(head, LANES // 2, 1), rest)
        extra[at * PACK : (at + 1) * PACK] = first.astype(jnp.bfloat16)
        extra[(count + at) * PACK : (count + at + 1) * PACK] = second.astype(jnp.bfloat16)


def product_kernel(rows, grads, extra, out):
    units = grads.shape[1]

    def step(at, _):
        cols = pl.ds(pl.multiple_of(at * 256, 256), 256)
        out[:, cols] = jnp.dot(rows[...], grads[:, cols], preferred_element_type=jnp.float32).astype(jnp.bfloat16)
        return 0

    lax.fori_loop(0, units // 256, step, 0)
    out[:, units:] = extra[...]


def merge_kernel(*refs):
    parts, out = refs[:-1], refs[-1]
    units = out.shape[1] - LANES
    size = 32

    def step(at, _):
        place = pl.ds(pl.multiple_of(at * size, size), size)
        wide = [part for part in parts if part.shape[1] > units]
        plain = [part for part in parts if part.shape[1] == units]
        packed = added(*[part[place, units:] for part in wide])
        out[place, units:] = paired(packed).astype(jnp.bfloat16)
        if len(plain) == 2:
            wide = wide[1:]
        out[place, :units] = added(*[part[place, :units] for part in wide + plain]).astype(jnp.bfloat16)
        return 0

    lax.fori_loop(0, out.shape[0] // size, step, 0)


def piece_kernel(parts, out):
    units = out.shape[1] - LANES
    total = parts[0].astype(jnp.float32)
    for at in range(1, parts.shape[0]):
        total = total + parts[at].astype(jnp.float32)
    out[:, :units] = total[:, :units].astype(jnp.bfloat16)
    out[:, units:] = paired(total[:, units:]).astype(jnp.bfloat16)


def place_kernel(place, q0, q1, q2, q3, out, *, factor):
    rows = q0.shape[0]
    for step, part in enumerate((q0, q1, q2, q3)):
        start = pl.multiple_of((place[0] + 4 - step) % 4 * rows, rows)
        out[pl.ds(start, rows)] = part[...].astype(jnp.float32) * factor


def small_kernel(place, q0, q1, q2, q3, w0, w1, w2, w3, taps_out, table_out, packed, sums, *, factor):
    rows = q0.shape[0]
    for step, part in enumerate((q0, q1, q2, q3)):
        start = pl.multiple_of((place[0] + 4 - step) % 4 * rows, rows)
        packed[pl.ds(start, rows)] = part[...].astype(jnp.float32)
    cells = packed[...]
    whole = cells + pltpu.roll(cells, LANES // 2, 1)
    half = whole.shape[0] // 2
    whole = jnp.where(low_lanes((half, LANES)), whole[:half], whole[half:]) * factor
    count = half // PACK
    for at in range(count):
        cols = slice(at * LANES, (at + 1) * LANES)
        taps_out[:, cols] = whole[at * PACK : at * PACK + TAPS]
        sums[:, cols] = whole[at * PACK + 8 : at * PACK + 24]
    split = thirds(sums[...])
    dims = (((1,), (1,)), ((), ()))
    width = w0.shape[0]
    turn = turning(width)
    backs = []
    for w in (w0, w1, w2, w3):
        back = lax.dot_general(split, w[...], dims, preferred_element_type=jnp.float32)
        backs.append(back[:16] + back[16:32] + back[32:])
    for r in range(4):
        turned = jnp.dot(thirds(backs[r ^ 3][8:]), turn, preferred_element_type=jnp.float32)
        turned = turned[:8] + turned[8:16] + turned[16:]
        start = pl.multiple_of((place[1] ^ r) * width, width)
        table_out[:, pl.ds(start, width)] = (backs[r][:8] + turned)[: table_out.shape[0]]


def call(kernel, outs, *args, scratch=(), scalar=False):
    inside = pl.BlockSpec(memory_space=pltpu.VMEM)
    specs = [inside] * len(args)
    if scalar:
        specs[0] = pl.BlockSpec(memory_space=pltpu.SMEM)
    return pl.pallas_call(
        kernel,
        out_shape=outs,
        in_specs=specs,
        out_specs=jax.tree.map(lambda _: inside, outs),
        scratch_shapes=list(scratch),
        compiler_params=pltpu.CompilerParams(vmem_limit_bytes=48 * 2**20),
    )(*args)


def array(shape, dtype=jnp.bfloat16):
    return jax.ShapeDtypeStruct(shape, dtype)


def merged(*parts):
    rows = parts[0].shape[0]
    return call(merge_kernel, array((rows, max(part.shape[1] for part in parts))), *parts)


def reduce_rows(own, mate, side, side_mate):
    side_sum = merged(side, swap_core(side_mate))
    from_side = shift(side_sum, ("xl", "c", "xh"), side_x)
    block = merged(side_sum, from_side, own, swap_core(mate))
    y = lax.axis_index("y")
    rows = block.shape[0] // 4
    units = own.shape[1]
    parts = [lax.dynamic_slice_in_dim(block, y * rows, rows, 0)]
    for step in (1, 2, 3):
        chunk = lax.dynamic_slice_in_dim(block, (y + step) % 4 * rows, rows, 0)
        parts.append(shift(chunk, ("y",), lambda a: ((a + step) % 4,)))
    quarter = merged(*parts)
    pieces = quarter.reshape(16, rows // 16, -1)
    pieces = lax.all_to_all(pieces, ("xh", "z"), split_axis=0, concat_axis=0, tiled=True)
    piece = call(piece_kernel, array(pieces.shape[1:]), pieces)
    pieces = lax.all_to_all(
        jnp.broadcast_to(piece[None], pieces.shape), ("xh", "z"), split_axis=0, concat_axis=0, tiled=True
    )
    quarter = pieces.reshape(rows, -1)
    large = quarter[:, :units]
    small = quarter[:, units:]
    large = [large] + [shift(large, ("y",), lambda a: ((a + step) % 4,)) for step in (1, 2, 3)]
    small = [small] + [shift(small, ("y",), lambda a: ((a + step) % 4,)) for step in (1, 2, 3)]
    return large, small


def local(hidden, tokens, embedding, weight, kernel, cotangent):
    window = hidden[0]
    token_codes = tokens[0]
    upstream = cotangent[0]
    rows, features = window.shape
    units = weight.shape[1]
    factor = 1.0 / math.sqrt(rows * 256)
    width = features // 4
    me = 2 * lax.axis_index("xl") + lax.axis_index("c")
    blocks = [me ^ r for r in range(4)]
    weights = [weight, swap_core(weight), shift(weight, ("xl", "c", "xh"), side_x)]
    weights.append(swap_core(weights[2]))

    looked = jnp.zeros((rows, features), jnp.float32)
    for symbol in range(embedding.shape[0]):
        looked = looked + jnp.where((token_codes == symbol)[:, None], embedding[symbol][None, :], 0.0)
    stream = (window.astype(jnp.float32) + looked).astype(jnp.bfloat16)
    both = jnp.concatenate([stream, upstream], axis=1)
    before = shift(both[rows - EDGE :], ("xh", "z", "y"), neighbour(1))
    after = shift(both[:EDGE], ("xh", "z", "y"), neighbour(-1))
    wide = jnp.concatenate([before, both, after], axis=0)
    total = rows + 2 * EDGE

    def exchange(size):
        return (
            lax.broadcasted_iota(jnp.int32, (size, size), 0) + lax.broadcasted_iota(jnp.int32, (size, size), 1)
            == size - 1
        ).astype(jnp.bfloat16)

    def flipped(cells):
        size = 256
        count = cells.shape[1] // size
        turn = exchange(size)
        return jnp.concatenate(
            [
                jnp.dot(
                    cells[:, (count - 1 - at) * size : (count - at) * size],
                    turn,
                    preferred_element_type=jnp.float32,
                ).astype(jnp.bfloat16)
                for at in range(count)
            ],
            axis=1,
        )

    forward = [lax.dynamic_slice_in_dim(wide, at * width, width, 1) for at in blocks]
    reverse = [flipped(forward[r ^ 3]) for r in range(4)]
    stacks = [jnp.concatenate([forward[r], reverse[r]], axis=0) for r in range(4)]
    ups = wide[:, features:]
    ups = jnp.concatenate([ups, flipped(ups)], axis=0)
    hot = (jnp.arange(16, dtype=jnp.int32)[:, None] == token_codes[None, :]).astype(jnp.bfloat16)
    mid = slice(EDGE, EDGE + rows)
    columns = [jnp.concatenate([forward[r][mid], reverse[r][mid]], axis=0).T for r in range(4)]
    block_result, grad_stack, extra = call(
        strand_kernel,
        (array((rows, units)), array((2 * rows, units)), array((512, LANES))),
        jnp.stack(stacks),
        *weights,
        ups,
        kernel,
        hot,
        scratch=(
            pltpu.VMEM((2 * total, units), jnp.float32),
            pltpu.VMEM((2, total, LANES), jnp.float32),
            pltpu.VMEM((8, units), jnp.float32),
        ),
    )
    products = [
        jnp.dot(columns[r], grad_stack, preferred_element_type=jnp.float32).astype(jnp.bfloat16) for r in range(2)
    ]
    for r in (2, 3):
        products.append(call(product_kernel, array((width, units + LANES)), columns[r], grad_stack, extra))
    large, small = reduce_rows(*products)
    place = jnp.stack([lax.axis_index("y"), me]).astype(jnp.int32)
    grad_weight = call(
        functools.partial(place_kernel, factor=factor), array((width, units), jnp.float32), place, *large, scalar=True
    )
    grad_kernel, grad_embedding = call(
        functools.partial(small_kernel, factor=factor),
        (array(kernel.shape, jnp.float32), array(embedding.shape, jnp.float32)),
        place,
        *small,
        *weights,
        scalar=True,
        scratch=(pltpu.VMEM((512, LANES), jnp.float32), pltpu.VMEM((16, units), jnp.float32)),
    )
    backs = [
        lax.dot_general(grad_stack, weights[r], (((1,), (1,)), ((), ())), preferred_element_type=jnp.float32)
        for r in range(4)
    ]
    streams = jnp.stack(
        [backs[r][:rows] + flipped(backs[r ^ 3][rows:].astype(jnp.bfloat16)).astype(jnp.float32) for r in range(4)]
    )
    grad_stream = jnp.concatenate([streams[at ^ me] for at in range(4)], axis=1)
    return (
        block_result[None],
        grad_stream.astype(jnp.bfloat16)[None],
        grad_weight,
        grad_kernel,
        grad_embedding,
    )


def solution(mesh):
    fine = Mesh(mesh.devices.reshape(SIZES), AXES)
    batch = ("xl", "c")
    place = ("xh", "z", "y")
    in_specs = (P(batch, place, None), P(batch, place), P(), P(batch, None), P(), P(batch, place, None))
    out_specs = (P(batch, place, None), P(batch, place, None), P(batch, None), P(), P())
    return jax.shard_map(local, mesh=fine, in_specs=in_specs, out_specs=out_specs, check_vma=False)
```

```python
import functools
import math

import jax
import jax.numpy as jnp
import numpy as np
from jax import lax
from jax.experimental import pallas as pl
from jax.experimental.pallas import tpu as pltpu
from jax.sharding import Mesh, PartitionSpec as P


AXES = ("xl", "c", "xh", "z", "y")
SIZES = (2, 2, 2, 8, 4)
EDGE = 8
REACH = 3
TAPS = 7
LANES = 128
PACK = 32


def shift(cells, axes, target):
    sizes = [SIZES[AXES.index(axis)] for axis in axes]
    pairs = []
    for place in np.ndindex(*sizes):
        goal = target(*place)
        if goal is not None:
            pairs.append((int(np.ravel_multi_index(place, sizes)), int(np.ravel_multi_index(goal, sizes))))
    return lax.ppermute(cells, axes if len(axes) > 1 else axes[0], pairs)


def swap_core(cells):
    return shift(cells, ("c",), lambda c: (1 - c,))


def side(cells):
    def target(xl, c, xh):
        x = (2 * xh + xl + (1 if c == 0 else 3)) % 4
        return (x % 2, c, x // 2)

    return shift(cells, ("xl", "c", "xh"), target)


def along_y(cells, step):
    return shift(cells, ("y",), lambda y: ((y + step) % 4,))


def neighbour(step):
    def target(xh, z, y):
        place = (xh * 8 + z) * 4 + y + step
        if not 0 <= place < 64:
            return None
        return (place // 32, place // 4 % 8, place % 4)

    return target


def added(*parts):
    total = parts[0].astype(jnp.float32)
    for part in parts[1:]:
        total = total + part.astype(jnp.float32)
    return total


def low_lanes(shape):
    return lax.broadcasted_iota(jnp.int32, shape, len(shape) - 1) < LANES // 2


def paired(cells):
    whole = cells + pltpu.roll(cells, LANES // 2, 1)
    head = whole.astype(jnp.bfloat16).astype(jnp.float32)
    return jnp.where(low_lanes(cells.shape), head, whole - head)


def thirds(cells):
    head = cells.astype(jnp.bfloat16)
    rest = cells - head.astype(jnp.float32)
    middle = rest.astype(jnp.bfloat16)
    return head, middle, (rest - middle.astype(jnp.float32)).astype(jnp.bfloat16)


def turning(size):
    place = lax.broadcasted_iota(jnp.int32, (size, size), 0) + lax.broadcasted_iota(jnp.int32, (size, size), 1)
    return (place == size - 1).astype(jnp.bfloat16)


def dot(a, b):
    return jnp.dot(a, b, preferred_element_type=jnp.float32)


def turned(cells, turn):
    size = turn.shape[0]
    count = cells.shape[1] // size
    return jnp.concatenate([dot(cells[:, at * size : (at + 1) * size], turn) for at in range(count)[::-1]], axis=1)


def ready_kernel(place, window, codes, table, before, after, upstream, stacks, columns, ups):
    rows, features = window.shape
    width = features // 4
    total = rows + 2 * EDGE
    turn = turning(256)
    for r in range(4):
        cols = pl.ds(pl.multiple_of((place[0] ^ r) * width, width), width)
        looked = jnp.zeros((rows, width), jnp.float32)
        for symbol in range(table.shape[0]):
            looked = looked + jnp.where(codes[...] == symbol, table[symbol : symbol + 1, cols], 0.0)
        middle = (window[:, cols].astype(jnp.float32) + looked).astype(jnp.bfloat16)
        whole = jnp.concatenate(
            [
                before[:, cols].astype(jnp.float32),
                middle.astype(jnp.float32),
                after[:, cols].astype(jnp.float32),
            ],
            axis=0,
        ).astype(jnp.bfloat16)
        back = turned(whole, turn)
        stacks[r, :total] = whole
        stacks[3 - r, total:] = back.astype(jnp.bfloat16)
        columns[r, :, :rows] = middle.astype(jnp.float32).T.astype(jnp.bfloat16)
        columns[3 - r, :, rows:] = back[EDGE : EDGE + rows].T.astype(jnp.bfloat16)
    whole = jnp.concatenate(
        [
            before[:, features:].astype(jnp.float32),
            upstream[...].astype(jnp.float32),
            after[:, features:].astype(jnp.float32),
        ],
        axis=0,
    ).astype(jnp.bfloat16)
    ups[:total] = whole
    ups[total:] = turned(whole, turn).astype(jnp.bfloat16)


def strand_kernel(stacks, w0, w1, w2, w3, ups, taps, out, grads, sums, values, mixes):
    total = stacks.shape[1] // 2
    rows = total - 2 * EDGE
    units = w0.shape[1]
    count = units // LANES

    def project(at, _):
        cols = pl.ds(pl.multiple_of(at * 256, 256), 256)
        acc = jnp.zeros((2 * total, 256), jnp.float32)
        for r, w in enumerate((w0, w1, w2, w3)):
            acc = acc + dot(stacks[r], w[:, cols])
        values[:, cols] = acc.astype(jnp.bfloat16).astype(jnp.float32)
        return 0

    lax.fori_loop(0, units // 256, project, 0)
    sums[...] = jnp.zeros(sums.shape, jnp.float32)
    turn = turning(LANES)

    def work(at, _):
        outs = []
        for way in range(2):
            block = at if way == 0 else count - 1 - at
            cols = pl.ds(pl.multiple_of(block * LANES, LANES), LANES)
            base = way * total
            places = [base + EDGE + (tap - REACH if way == 0 else REACH - tap) for tap in range(TAPS)]
            linear = values[base : base + total, cols]
            logistic = jax.nn.sigmoid(linear)
            gating = linear * logistic
            up = ups[base : base + total, cols].astype(jnp.float32)
            grad_mix = up * gating
            mixes[way] = grad_mix
            mid = slice(EDGE, EDGE + rows)
            linear, logistic, gating, up, grad_mix = [
                cells[mid] for cells in (linear, logistic, gating, up, grad_mix)
            ]
            mixing = jnp.zeros((rows, LANES), jnp.float32)
            for tap in range(TAPS):
                moved = values[places[tap] : places[tap] + rows, cols]
                mixing = mixing + taps[tap : tap + 1, cols] * moved
                sums[tap : tap + 1, cols] += jnp.sum(grad_mix * moved, axis=0, keepdims=True)
            outs.append(mixing * gating)
            acc = up * mixing * logistic * (1.0 + linear * (1.0 - logistic))
            for tap in range(TAPS):
                lower = 2 * EDGE - places[tap] + base
                acc = acc + taps[tap : tap + 1, cols] * mixes[way, lower : lower + rows]
            grads[way * rows : (way + 1) * rows, cols] = acc.astype(jnp.bfloat16)
        out[:, pl.ds(pl.multiple_of(at * LANES, LANES), LANES)] = (
            outs[0] + dot(outs[1].astype(jnp.bfloat16), turn)
        ).astype(jnp.bfloat16)
        return 0

    lax.fori_loop(0, count, work, 0)


def product_kernel(columns, grads, out, *, block, start):
    out[...] = dot(columns[block, start : start + out.shape[0]], grads[...]).astype(jnp.bfloat16)


def later_product_kernel(columns, grads, earlier, out, *, block, start):
    product_kernel(columns, grads, out, block=block, start=start)


def side_kernel(columns, grads, came, out, *, block, start):
    own = dot(columns[block, start : start + out.shape[0]], grads[...])
    out[...] = (own + came[...].astype(jnp.float32)).astype(jnp.bfloat16)


def back_kernel(place, grads, hot, sums, w0, w1, w2, w3, later, out, packed, table):
    rows = out.shape[0]
    width = w0.shape[0]
    turn = turning(256)
    dims = (((1,), (1,)), ((), ()))
    weights = (w0, w1, w2, w3)
    for r in range(4):
        here = lax.dot_general(grads[:rows], weights[r][...], dims, preferred_element_type=jnp.float32)
        there = lax.dot_general(grads[rows:], weights[3 - r][...], dims, preferred_element_type=jnp.float32)
        whole = here + turned(there.astype(jnp.bfloat16), turn)
        cols = pl.ds(pl.multiple_of((place[0] ^ r) * width, width), width)
        out[:, cols] = whole.astype(jnp.bfloat16)
        table[:, cols] = added(*[dot(hot[...], part) for part in thirds(whole)])
    count = sums.shape[1] // LANES
    half = table.shape[1] // 2
    for at in range(count):
        cols = slice(at * LANES, (at + 1) * LANES)
        packed[at * PACK : at * PACK + 8] = sums[:, cols]
        packed[at * PACK + 8 : at * PACK + 16] = table[:8, cols]
        packed[at * PACK + 16 : at * PACK + 24] = table[:8, half + at * LANES : half + (at + 1) * LANES]
        packed[at * PACK + 24 : at * PACK + 32] = jnp.zeros((8, LANES), jnp.float32)


def block_kernel(place, columns, grads, mate, came, *refs, start):
    if len(refs) > 4:
        packed, packed_came, outs, first, second = refs[0], refs[1], refs[2:6], refs[6], refs[7]
        whole = packed[...] + packed_came[...]
        head = whole.astype(jnp.bfloat16).astype(jnp.float32)
        rest = whole - head
        low = low_lanes(whole.shape)
        first[...] = jnp.where(low, head, pltpu.roll(rest, LANES // 2, 1))
        second[...] = jnp.where(low, pltpu.roll(head, LANES // 2, 1), rest)
    else:
        outs = refs
    rows = outs[0].shape[0]
    units = grads.shape[1]
    for step, out in enumerate(outs):
        at = pl.multiple_of((place[1] + step) % 4 * rows, rows)
        own = dot(columns[0, pl.ds(start + at, rows)], grads[...])
        here = pl.ds(at, rows)
        out[:, :units] = (
            own + mate[pl.ds(start + at, rows)].astype(jnp.float32) + came[here].astype(jnp.float32)
        ).astype(jnp.bfloat16)
        if len(refs) > 4:
            out[:, units : units + LANES] = first[here].astype(jnp.bfloat16)
            out[:, units + LANES :] = second[here].astype(jnp.bfloat16)


def quarter_kernel(*refs):
    head, tail, out = refs[:4], refs[4:8], refs[8]
    rows, units = head[0].shape
    size = 16

    def step(at, _):
        here = pl.ds(pl.multiple_of(at * size, size), size)
        there = pl.ds(pl.multiple_of(rows + at * size, size), size)
        out[here, :units] = added(*[part[here] for part in head]).astype(jnp.bfloat16)
        out[there, :units] = added(*[part[here, :units] for part in tail]).astype(jnp.bfloat16)
        for goal, start in ((here, units), (there, units + LANES)):
            cells = added(*[part[here, start : start + LANES] for part in tail])
            out[goal, units:] = paired(cells).astype(jnp.bfloat16)
        return 0

    lax.fori_loop(0, rows // size, step, 0)


def piece_kernel(parts, out):
    units = out.shape[2] - LANES
    total = parts[0].astype(jnp.float32)
    for at in range(1, parts.shape[0]):
        total = total + parts[at].astype(jnp.float32)
    plain = total[:, :units].astype(jnp.bfloat16)
    packed = paired(total[:, units:]).astype(jnp.bfloat16)
    for at in range(parts.shape[0]):
        out[at, :, :units] = plain
        out[at, :, units:] = packed


def final_kernel(place, q0, q1, q2, q3, weight_out, taps_out, table_out, packed, *, factor):
    rows = q0.shape[0] // 2
    units = weight_out.shape[1]
    for step, part in enumerate((q0, q1, q2, q3)):
        at = pl.multiple_of((place[1] + 4 - step) % 4 * rows, rows)
        for half in range(2):
            here = slice(half * rows, (half + 1) * rows)
            there = pl.ds(half * 4 * rows + at, rows)
            weight_out[there] = part[here, :units].astype(jnp.float32) * factor
            packed[there] = part[here, units:].astype(jnp.float32)
    cells = packed[...]
    whole = cells + pltpu.roll(cells, LANES // 2, 1)
    half = whole.shape[0] // 2
    whole = jnp.where(low_lanes((half, LANES)), whole[:half], whole[half:]) * factor
    count = half // PACK
    symbols = table_out.shape[0]
    for at in range(count):
        cols = slice(at * LANES, (at + 1) * LANES)
        taps_out[:, cols] = whole[at * PACK : at * PACK + TAPS]
        table_out[:, cols] = whole[at * PACK + 8 : at * PACK + 8 + symbols]
        cols = slice(units + at * LANES, units + (at + 1) * LANES)
        table_out[:, cols] = whole[at * PACK + 16 : at * PACK + 16 + symbols]


def call(kernel, outs, *args, scratch=(), scalar=False, unread=None, **fixed):
    inside = pl.BlockSpec(memory_space=pltpu.VMEM)
    specs = [inside] * len(args)
    if scalar:
        specs[0] = pl.BlockSpec(memory_space=pltpu.SMEM)
    if unread is not None:
        specs[unread] = pl.BlockSpec(memory_space=pl.ANY)
    return pl.pallas_call(
        functools.partial(kernel, **fixed),
        out_shape=outs,
        in_specs=specs,
        out_specs=jax.tree.map(lambda _: inside, outs),
        scratch_shapes=list(scratch),
        compiler_params=pltpu.CompilerParams(vmem_limit_bytes=20 * 2**20),
    )(*args)


def array(shape, dtype=jnp.bfloat16):
    return jax.ShapeDtypeStruct(shape, dtype)


def step(hidden, tokens, embedding, weight, kernel, cotangent):
    window = hidden[0]
    upstream = cotangent[0]
    rows, features = window.shape
    units = weight.shape[1]
    symbols = embedding.shape[0]
    factor = 1.0 / math.sqrt(rows * 256)
    width = features // 4
    total = rows + 2 * EDGE
    me = 2 * lax.axis_index("xl") + lax.axis_index("c")
    place = jnp.stack([me, lax.axis_index("y")]).astype(jnp.int32)
    weights = [weight, swap_core(weight), side(weight)]
    weights.append(swap_core(weights[2]))
    codes = tokens[0][:, None]

    def edge(part):
        looked = jnp.zeros((EDGE, features), jnp.float32)
        for symbol in range(symbols):
            looked = looked + jnp.where(codes[part] == symbol, embedding[symbol][None, :], 0.0)
        stream = (window[part].astype(jnp.float32) + looked).astype(jnp.bfloat16)
        return jnp.concatenate([stream, upstream[part]], axis=1)

    before = shift(edge(slice(rows - EDGE, rows)), ("xh", "z", "y"), neighbour(1))
    after = shift(edge(slice(0, EDGE)), ("xh", "z", "y"), neighbour(-1))
    stacks, columns, ups = call(
        ready_kernel,
        (array((4, 2 * total, width)), array((4, width, 2 * rows)), array((2 * total, units))),
        place,
        window,
        codes,
        embedding,
        before,
        after,
        upstream,
        scalar=True,
    )
    block_result, grads, sums = call(
        strand_kernel,
        (array((rows, units)), array((2 * rows, units)), array((8, units), jnp.float32)),
        stacks,
        *weights,
        ups,
        kernel,
        scratch=(pltpu.VMEM((2 * total, units), jnp.float32), pltpu.VMEM((2, total, LANES), jnp.float32)),
    )

    half = width // 2
    chunk = array((half, units))
    goes = call(product_kernel, chunk, columns, grads, block=3, start=0)
    goes = [goes, call(later_product_kernel, chunk, columns, grads, goes, unread=2, block=3, start=half)]
    mate = call(later_product_kernel, array((width, units)), columns, grads, goes[1], unread=2, block=1, start=0)
    came = [swap_core(goes[at]) for at in range(2)]
    mate = swap_core(mate)
    sides = [call(side_kernel, chunk, columns, grads, came[at], block=2, start=at * half) for at in range(2)]
    came = [side(sides[at]) for at in range(2)]
    hot = (jnp.arange(16, dtype=jnp.int32)[:, None] == tokens).astype(jnp.bfloat16)
    grad_hidden, packed = call(
        back_kernel,
        (array((rows, features)), array((units // LANES * PACK, LANES), jnp.float32)),
        place,
        grads,
        hot,
        sums,
        *weights,
        sides[1],
        scalar=True,
        unread=8,
        scratch=(pltpu.VMEM((16, features), jnp.float32),),
    )
    packed = packed + swap_core(packed)
    part = half // 4
    head = call(block_kernel, (array((part, units)),) * 4, place, columns, grads, mate, came[0], scalar=True, start=0)
    head = [head[0]] + [along_y(head[step], step) for step in (1, 2, 3)]
    tail = call(
        block_kernel,
        (array((part, units + 2 * LANES)),) * 4,
        place,
        columns,
        grads,
        mate,
        came[1],
        packed,
        side(packed),
        scalar=True,
        scratch=(pltpu.VMEM(packed.shape, jnp.float32),) * 2,
        start=half,
    )
    tail = [tail[0]] + [along_y(tail[step], step) for step in (1, 2, 3)]
    quarter = call(quarter_kernel, array((2 * part, units + LANES)), *head, *tail)
    pieces = quarter.reshape(16, part // 8, -1)
    pieces = lax.all_to_all(pieces, ("xh", "z"), split_axis=0, concat_axis=0, tiled=True)
    pieces = call(piece_kernel, array(pieces.shape), pieces)
    pieces = lax.all_to_all(pieces, ("xh", "z"), split_axis=0, concat_axis=0, tiled=True)
    quarter = pieces.reshape(quarter.shape)
    quarters = [quarter] + [along_y(quarter, step) for step in (1, 2, 3)]
    grad_weight, grad_kernel, grad_embedding = call(
        final_kernel,
        (array((width, units), jnp.float32), array(kernel.shape, jnp.float32), array(embedding.shape, jnp.float32)),
        place,
        *quarters,
        scalar=True,
        scratch=(pltpu.VMEM((width, LANES), jnp.float32),),
        factor=factor,
    )
    return block_result[None], grad_hidden[None], grad_weight, grad_kernel, grad_embedding


def solution(mesh):
    fine = Mesh(mesh.devices.reshape(SIZES), AXES)
    batch = ("xl", "c")
    spot = ("xh", "z", "y")
    in_specs = (P(batch, spot, None), P(batch, spot), P(), P(batch, None), P(), P(batch, spot, None))
    out_specs = (P(batch, spot, None), P(batch, spot, None), P(batch, None), P(), P())
    return jax.shard_map(step, mesh=fine, in_specs=in_specs, out_specs=out_specs, check_vma=False)
```

```python
import functools
import math

import jax
import jax.numpy as jnp
import numpy as np
from jax import lax
from jax.experimental import pallas as pl
from jax.experimental.pallas import tpu as pltpu
from jax.sharding import Mesh, PartitionSpec as P


AXES = ("xl", "c", "xh", "z", "y")
SIZES = (2, 2, 2, 8, 4)
EDGE = 8
REACH = 3
TAPS = 7
LANES = 128
PACK = 32


def shift(cells, axes, target):
    sizes = [SIZES[AXES.index(axis)] for axis in axes]
    pairs = []
    for place in np.ndindex(*sizes):
        goal = target(*place)
        if goal is not None:
            pairs.append((int(np.ravel_multi_index(place, sizes)), int(np.ravel_multi_index(goal, sizes))))
    return lax.ppermute(cells, axes if len(axes) > 1 else axes[0], pairs)


def swap_core(cells):
    return shift(cells, ("c",), lambda c: (1 - c,))


def side(cells):
    def target(xl, c, xh):
        x = (2 * xh + xl + (1 if c == 0 else 3)) % 4
        return (x % 2, c, x // 2)

    return shift(cells, ("xl", "c", "xh"), target)


def along_y(cells, step):
    return shift(cells, ("y",), lambda y: ((y + step) % 4,))


def neighbour(step):
    def target(xh, z, y):
        place = (xh * 8 + z) * 4 + y + step
        if not 0 <= place < 64:
            return None
        return (place // 32, place // 4 % 8, place % 4)

    return target


def added(*parts):
    total = parts[0].astype(jnp.float32)
    for part in parts[1:]:
        total = total + part.astype(jnp.float32)
    return total


def low_lanes(shape):
    return lax.broadcasted_iota(jnp.int32, shape, len(shape) - 1) < LANES // 2


def paired(cells):
    whole = cells + pltpu.roll(cells, LANES // 2, 1)
    head = whole.astype(jnp.bfloat16).astype(jnp.float32)
    return jnp.where(low_lanes(cells.shape), head, whole - head)


def thirds(cells):
    head = cells.astype(jnp.bfloat16)
    rest = cells - head.astype(jnp.float32)
    middle = rest.astype(jnp.bfloat16)
    return head, middle, (rest - middle.astype(jnp.float32)).astype(jnp.bfloat16)


def turning(size):
    place = lax.broadcasted_iota(jnp.int32, (size, size), 0) + lax.broadcasted_iota(jnp.int32, (size, size), 1)
    return (place == size - 1).astype(jnp.bfloat16)


def dot(a, b):
    return jnp.dot(a, b, preferred_element_type=jnp.float32)


def turned(cells, turn):
    size = turn.shape[0]
    count = cells.shape[1] // size
    return jnp.concatenate([dot(cells[:, at * size : (at + 1) * size], turn) for at in range(count)[::-1]], axis=1)


def edge_kernel(codes, last, first, up_last, up_first, table, before, after, looked):
    rows = codes.shape[1]
    features = table.shape[1]
    for start, cells, up, out in ((rows - EDGE, last, up_last, before), (0, first, up_first, after)):
        for at in range(EDGE):
            looked[at : at + 1] = table[pl.ds(codes[0, start + at], 1)]
        out[:, :features] = (cells[...].astype(jnp.float32) + looked[...]).astype(jnp.bfloat16)
        out[:, features:] = up[...]


def centre_kernel(
    place, codes, taps, window_far, table_far, up_far, stacks, columns, ups, taps_near, hot, window, table, up, done
):
    loads = [
        pltpu.make_async_copy(far, near, done.at[at])
        for at, (far, near) in enumerate(((window_far, window), (table_far, table), (up_far, up)))
    ]
    for load in loads:
        load.start()
    taps_near[...] = taps[...]
    rows, features = window.shape
    symbol = lax.broadcasted_iota(jnp.int32, (16, rows), 0)
    one_hot = jnp.where(symbol == codes[...], 1.0, 0.0).astype(jnp.bfloat16)
    for at in range(3):
        hot[:, at * rows : (at + 1) * rows] = one_hot
    width = features // 4
    turn = turning(256)
    by_row = jnp.broadcast_to(codes[...].astype(jnp.float32), (rows, rows)).T
    by_row = jnp.concatenate([by_row] * (width // rows), axis=1)
    for load in loads:
        load.wait()
    for r in range(4):
        cols = pl.ds(pl.multiple_of((place[0] ^ r) * width, width), width)
        looked = jnp.zeros((rows, width), jnp.float32)
        for symbol in range(table.shape[0]):
            looked = looked + jnp.where(by_row == symbol, table[symbol : symbol + 1, cols], 0.0)
        middle = (window[:, cols].astype(jnp.float32) + looked).astype(jnp.bfloat16)
        back = turned(middle, turn)
        stacks[r, :rows] = middle
        stacks[3 - r, rows:] = back.astype(jnp.bfloat16)
        columns[r, :, :rows] = middle.astype(jnp.float32).T.astype(jnp.bfloat16)
        columns[3 - r, :, rows:] = back.T.astype(jnp.bfloat16)
    ups[:rows] = up[...].astype(jnp.float32)
    ups[rows:] = turned(up[...], turn)


def early_kernel(place, centre, up_centre, before, after, w0, w1, stacks, ups, partial):
    rows = up_centre.shape[0] // 2
    features = 4 * centre.shape[2]
    width = centre.shape[2]
    total = rows + 2 * EDGE
    turn = turning(256)
    for r in range(4):
        cols = pl.ds(pl.multiple_of((place[0] ^ r) * width, width), width)
        halo = jnp.concatenate([before[:, cols].astype(jnp.float32), after[:, cols].astype(jnp.float32)], axis=0)
        halo = halo.astype(jnp.bfloat16)
        stacks[r, : 2 * rows] = centre[r]
        stacks[r, 2 * rows : 2 * rows + 2 * EDGE] = halo
        stacks[3 - r, 2 * rows + 2 * EDGE :] = turned(halo, turn).astype(jnp.bfloat16)
    for way in range(2):
        base = way * total
        ups[base + EDGE : base + EDGE + rows] = up_centre[way * rows : (way + 1) * rows]
        for part, start in ((before, base), (after, base + EDGE + rows)):
            cells = part[:, features:].astype(jnp.float32)
            if way == 1:
                cells = turned(cells.astype(jnp.bfloat16), turn)
            ups[start : start + EDGE] = cells
    add_products(partial, None, ((stacks.at[0], w0), (stacks.at[1], w1)))


def add_products(out, start, pairs):
    def step(at, _):
        cols = pl.ds(pl.multiple_of(at * 256, 256), 256)
        acc = added(*[dot(cells[...], w[:, cols]) for cells, w in pairs])
        if start is not None:
            acc = acc + start[:, cols]
        out[:, cols] = acc
        return 0

    lax.fori_loop(0, out.shape[1] // 256, step, 0)


def middle_kernel(stacks, partial, w2, out):
    add_products(out, partial, ((stacks.at[2], w2),))


def strand_kernel(stacks, partial, w3, ups, taps, out, grads, sums, values, mixes):
    total = stacks.shape[1] // 2
    rows = total - 2 * EDGE
    units = w3.shape[1]
    count = units // LANES

    def project(at, _):
        cols = pl.ds(pl.multiple_of(at * 256, 256), 256)
        acc = partial[:, cols] + dot(stacks[3], w3[:, cols])
        acc = acc.astype(jnp.bfloat16).astype(jnp.float32)
        for way in range(2):
            base = way * total
            halo = 2 * rows + way * 2 * EDGE
            values[base : base + EDGE, cols] = acc[halo : halo + EDGE]
            values[base + EDGE : base + EDGE + rows, cols] = acc[way * rows : (way + 1) * rows]
            values[base + EDGE + rows : base + total, cols] = acc[halo + EDGE : halo + 2 * EDGE]
        return 0

    lax.fori_loop(0, units // 256, project, 0)
    sums[...] = jnp.zeros(sums.shape, jnp.float32)
    turn = turning(LANES)

    def work(at, _):
        outs = []
        for way in range(2):
            block = at if way == 0 else count - 1 - at
            cols = pl.ds(pl.multiple_of(block * LANES, LANES), LANES)
            base = way * total
            places = [base + EDGE + (tap - REACH if way == 0 else REACH - tap) for tap in range(TAPS)]
            linear = values[base : base + total, cols]
            logistic = jax.nn.sigmoid(linear)
            gating = linear * logistic
            up = ups[base : base + total, cols]
            grad_mix = up * gating
            mixes[way] = grad_mix
            mid = slice(EDGE, EDGE + rows)
            linear, logistic, gating, up, grad_mix = [
                cells[mid] for cells in (linear, logistic, gating, up, grad_mix)
            ]
            mixing = jnp.zeros((rows, LANES), jnp.float32)
            for tap in range(TAPS):
                moved = values[places[tap] : places[tap] + rows, cols]
                mixing = mixing + taps[tap : tap + 1, cols] * moved
                sums[tap : tap + 1, cols] += jnp.sum(grad_mix * moved, axis=0, keepdims=True)
            outs.append(mixing * gating)
            acc = up * mixing * logistic * (1.0 + linear * (1.0 - logistic))
            for tap in range(TAPS):
                lower = 2 * EDGE - places[tap] + base
                acc = acc + taps[tap : tap + 1, cols] * mixes[way, lower : lower + rows]
            grads[way * rows : (way + 1) * rows, cols] = acc.astype(jnp.bfloat16)
        out[:, pl.ds(pl.multiple_of(at * LANES, LANES), LANES)] = (
            outs[0] + dot(outs[1].astype(jnp.bfloat16), turn)
        ).astype(jnp.bfloat16)
        return 0

    lax.fori_loop(0, count, work, 0)


def product_kernel(columns, grads, out, *, block, start):
    out[...] = dot(columns[block, start : start + out.shape[0]], grads[...]).astype(jnp.bfloat16)


def later_product_kernel(columns, grads, earlier, out, *, block, start):
    product_kernel(columns, grads, out, block=block, start=start)


def side_kernel(columns, grads, came, out, *, block, start):
    own = dot(columns[block, start : start + out.shape[0]], grads[...])
    out[...] = (own + came[...].astype(jnp.float32)).astype(jnp.bfloat16)


def back_kernel(place, grads, hot, sums, w0, w1, w2, w3, later, out, packed, table, backs):
    rows = out.shape[0]
    width = w0.shape[0]
    turn = turning(256)
    dims = (((1,), (1,)), ((), ()))
    for r, w in enumerate((w0, w1, w2, w3)):
        backs[r] = lax.dot_general(grads[...], w[...], dims, preferred_element_type=jnp.float32)
    for r in range(4):
        whole = backs[r, :rows] + turned(backs[3 - r, rows:].astype(jnp.bfloat16), turn)
        cols = pl.ds(pl.multiple_of((place[0] ^ r) * width, width), width)
        out[:, cols] = whole.astype(jnp.bfloat16)
        table[:, cols] = dot(hot[...], jnp.concatenate(thirds(whole), axis=0))
    count = sums.shape[1] // LANES
    half = table.shape[1] // 2
    for at in range(count):
        cols = slice(at * LANES, (at + 1) * LANES)
        packed[at * PACK : at * PACK + 8] = sums[:, cols]
        packed[at * PACK + 8 : at * PACK + 16] = table[:8, cols]
        packed[at * PACK + 16 : at * PACK + 24] = table[:8, half + at * LANES : half + (at + 1) * LANES]
        packed[at * PACK + 24 : at * PACK + 32] = jnp.zeros((8, LANES), jnp.float32)


def block_kernel(place, columns, grads, mate, came, *refs, start):
    wide = len(refs) > 5
    own = refs[-1]
    if wide:
        packed, packed_came, outs, first, second = refs[0], refs[1], refs[2:6], refs[6], refs[7]
        whole = packed[...] + packed_came[...]
        head = whole.astype(jnp.bfloat16).astype(jnp.float32)
        rest = whole - head
        low = low_lanes(whole.shape)
        first[...] = jnp.where(low, head, pltpu.roll(rest, LANES // 2, 1))
        second[...] = jnp.where(low, pltpu.roll(head, LANES // 2, 1), rest)
    else:
        outs = refs[:4]
    rows = outs[0].shape[0]
    units = grads.shape[1]
    own[...] = dot(columns[0, start : start + 4 * rows], grads[...])
    for step, out in enumerate(outs):
        at = pl.multiple_of((place[1] + step) % 4 * rows, rows)
        here = pl.ds(at, rows)
        out[:, :units] = added(own[here], mate[pl.ds(start + at, rows)], came[here]).astype(jnp.bfloat16)
        if wide:
            out[:, units : units + LANES] = first[here].astype(jnp.bfloat16)
            out[:, units + LANES :] = second[here].astype(jnp.bfloat16)


def quarter_kernel(*refs):
    head, tail, out = refs[:4], refs[4:8], refs[8]
    rows, units = head[0].shape
    size = 16

    def step(at, _):
        here = pl.ds(pl.multiple_of(at * size, size), size)
        there = pl.ds(pl.multiple_of(rows + at * size, size), size)
        out[here, :units] = added(*[part[here] for part in head]).astype(jnp.bfloat16)
        out[there, :units] = added(*[part[here, :units] for part in tail]).astype(jnp.bfloat16)
        for goal, start in ((here, units), (there, units + LANES)):
            cells = added(*[part[here, start : start + LANES] for part in tail])
            out[goal, units:] = paired(cells).astype(jnp.bfloat16)
        return 0

    lax.fori_loop(0, rows // size, step, 0)


def piece_kernel(parts, out):
    units = out.shape[2] - LANES
    total = parts[0].astype(jnp.float32)
    for at in range(1, parts.shape[0]):
        total = total + parts[at].astype(jnp.float32)
    plain = total[:, :units].astype(jnp.bfloat16)
    packed = paired(total[:, units:]).astype(jnp.bfloat16)
    for at in range(parts.shape[0]):
        out[at, :, :units] = plain
        out[at, :, units:] = packed


def final_kernel(place, q0, q1, q2, q3, weight_out, taps_out, table_out, packed, *, factor):
    rows = q0.shape[0] // 2
    units = weight_out.shape[1]
    for step, part in enumerate((q0, q1, q2, q3)):
        at = pl.multiple_of((place[1] + 4 - step) % 4 * rows, rows)
        for half in range(2):
            here = slice(half * rows, (half + 1) * rows)
            there = pl.ds(half * 4 * rows + at, rows)
            weight_out[there] = part[here, :units].astype(jnp.float32) * factor
            packed[there] = part[here, units:].astype(jnp.float32)
    cells = packed[...]
    whole = cells + pltpu.roll(cells, LANES // 2, 1)
    half = whole.shape[0] // 2
    whole = jnp.where(low_lanes((half, LANES)), whole[:half], whole[half:]) * factor
    count = half // PACK
    symbols = table_out.shape[0]
    for at in range(count):
        cols = slice(at * LANES, (at + 1) * LANES)
        taps_out[:, cols] = whole[at * PACK : at * PACK + TAPS]
        table_out[:, cols] = whole[at * PACK + 8 : at * PACK + 8 + symbols]
        cols = slice(units + at * LANES, units + (at + 1) * LANES)
        table_out[:, cols] = whole[at * PACK + 16 : at * PACK + 16 + symbols]


def call(kernel, outs, *args, scratch=(), scalar=False, unread=(), **fixed):
    inside = pl.BlockSpec(memory_space=pltpu.VMEM)
    specs = [inside] * len(args)
    if scalar:
        specs[0] = pl.BlockSpec(memory_space=pltpu.SMEM)
    for at in unread:
        specs[at] = pl.BlockSpec(memory_space=pl.ANY)
    return pl.pallas_call(
        functools.partial(kernel, **fixed),
        out_shape=outs,
        in_specs=specs,
        out_specs=jax.tree.map(lambda _: inside, outs),
        scratch_shapes=list(scratch),
        compiler_params=pltpu.CompilerParams(vmem_limit_bytes=20 * 2**20),
    )(*args)


def array(shape, dtype=jnp.bfloat16):
    return jax.ShapeDtypeStruct(shape, dtype)


def step(hidden, tokens, embedding, weight, kernel, cotangent):
    window = hidden[0]
    upstream = cotangent[0]
    rows, features = window.shape
    units = weight.shape[1]
    symbols = embedding.shape[0]
    factor = 1.0 / math.sqrt(rows * 256)
    width = features // 4
    total = rows + 2 * EDGE
    me = 2 * lax.axis_index("xl") + lax.axis_index("c")
    place = jnp.stack([me, lax.axis_index("y")]).astype(jnp.int32)
    weights = [weight, swap_core(weight), side(weight)]
    weights.append(swap_core(weights[2]))
    top = pl.BlockSpec((EDGE, features), lambda at: (0, 0))
    bottom = pl.BlockSpec((EDGE, features), lambda at: (rows // EDGE - 1, 0))
    up_top = pl.BlockSpec((EDGE, units), lambda at: (0, 0))
    up_bottom = pl.BlockSpec((EDGE, units), lambda at: (rows // EDGE - 1, 0))
    edge = array((EDGE, features + units))
    before, after = pl.pallas_call(
        edge_kernel,
        out_shape=(edge, edge),
        grid=(1,),
        in_specs=[
            pl.BlockSpec(memory_space=pltpu.SMEM),
            bottom,
            top,
            up_bottom,
            up_top,
            pl.BlockSpec((symbols, features), lambda at: (0, 0)),
        ],
        out_specs=[pl.BlockSpec(edge.shape, lambda at: (0, 0))] * 2,
        scratch_shapes=[pltpu.VMEM((EDGE, features), jnp.float32)],
    )(tokens, window, window, upstream, upstream, embedding)
    before = shift(before, ("xh", "z", "y"), neighbour(1))
    after = shift(after, ("xh", "z", "y"), neighbour(-1))
    centre, columns, up_centre, taps, hot = call(
        centre_kernel,
        (
            array((4, 2 * rows, width)),
            array((4, width, 2 * rows)),
            array((2 * rows, units), jnp.float32),
            array(kernel.shape, jnp.float32),
            array((16, 3 * rows)),
        ),
        place,
        tokens,
        kernel,
        window,
        embedding,
        upstream,
        scalar=True,
        unread=(3, 4, 5),
        scratch=(
            pltpu.VMEM((rows, features), jnp.bfloat16),
            pltpu.VMEM((symbols, features), jnp.float32),
            pltpu.VMEM((rows, units), jnp.bfloat16),
            pltpu.SemaphoreType.DMA((3,)),
        ),
    )
    wide = array((2 * total, units), jnp.float32)
    stacks, ups, partial = call(
        early_kernel,
        (array((4, 2 * total, width)), wide, wide),
        place,
        centre,
        up_centre,
        before,
        after,
        weights[0],
        weights[1],
        scalar=True,
    )
    partial = call(middle_kernel, wide, stacks, partial, weights[2])
    block_result, grads, sums = call(
        strand_kernel,
        (array((rows, units)), array((2 * rows, units)), array((8, units), jnp.float32)),
        stacks,
        partial,
        weights[3],
        ups,
        taps,
        scratch=(pltpu.VMEM((2 * total, units), jnp.float32), pltpu.VMEM((2, total, LANES), jnp.float32)),
    )

    half = width // 2
    chunk = array((half, units))
    goes = call(product_kernel, chunk, columns, grads, block=3, start=0)
    goes = [goes, call(later_product_kernel, chunk, columns, grads, goes, unread=(2,), block=3, start=half)]
    mate = call(later_product_kernel, array((width, units)), columns, grads, goes[1], unread=(2,), block=1, start=0)
    came = [swap_core(goes[at]) for at in range(2)]
    mate = swap_core(mate)
    sides = [call(side_kernel, chunk, columns, grads, came[at], block=2, start=at * half) for at in range(2)]
    came = [side(sides[at]) for at in range(2)]
    grad_hidden, packed = call(
        back_kernel,
        (array((rows, features)), array((units // LANES * PACK, LANES), jnp.float32)),
        place,
        grads,
        hot,
        sums,
        *weights,
        sides[1],
        scalar=True,
        unread=(8,),
        scratch=(pltpu.VMEM((16, features), jnp.float32), pltpu.VMEM((4, 2 * rows, width), jnp.float32)),
    )
    packed = packed + swap_core(packed)
    part = half // 4
    head = call(
        block_kernel,
        (array((part, units)),) * 4,
        place,
        columns,
        grads,
        mate,
        came[0],
        scalar=True,
        scratch=(pltpu.VMEM((half, units), jnp.float32),),
        start=0,
    )
    head = [head[0]] + [along_y(head[step], step) for step in (1, 2, 3)]
    tail = call(
        block_kernel,
        (array((part, units + 2 * LANES)),) * 4,
        place,
        columns,
        grads,
        mate,
        came[1],
        packed,
        side(packed),
        scalar=True,
        scratch=(pltpu.VMEM(packed.shape, jnp.float32),) * 2 + (pltpu.VMEM((half, units), jnp.float32),),
        start=half,
    )
    tail = [tail[0]] + [along_y(tail[step], step) for step in (1, 2, 3)]
    quarter = call(quarter_kernel, array((2 * part, units + LANES)), *head, *tail)
    pieces = quarter.reshape(16, part // 8, -1)
    pieces = lax.all_to_all(pieces, ("xh", "z"), split_axis=0, concat_axis=0, tiled=True)
    pieces = call(piece_kernel, array(pieces.shape), pieces)
    pieces = lax.all_to_all(pieces, ("xh", "z"), split_axis=0, concat_axis=0, tiled=True)
    quarter = pieces.reshape(quarter.shape)
    quarters = [quarter] + [along_y(quarter, step) for step in (1, 2, 3)]
    grad_weight, grad_kernel, grad_embedding = call(
        final_kernel,
        (array((width, units), jnp.float32), array(kernel.shape, jnp.float32), array(embedding.shape, jnp.float32)),
        place,
        *quarters,
        scalar=True,
        scratch=(pltpu.VMEM((width, LANES), jnp.float32),),
        factor=factor,
    )
    return block_result[None], grad_hidden[None], grad_weight, grad_kernel, grad_embedding


def solution(mesh):
    fine = Mesh(mesh.devices.reshape(SIZES), AXES)
    batch = ("xl", "c")
    spot = ("xh", "z", "y")
    in_specs = (P(batch, spot, None), P(batch, spot), P(), P(batch, None), P(), P(batch, spot, None))
    out_specs = (P(batch, spot, None), P(batch, spot, None), P(batch, None), P(), P())
    return jax.shard_map(step, mesh=fine, in_specs=in_specs, out_specs=out_specs, check_vma=False)
```

```python
import functools
import math

import jax
import jax.numpy as jnp
import numpy as np
from jax import lax
from jax.experimental import pallas as pl
from jax.experimental.pallas import tpu as pltpu
from jax.sharding import Mesh, PartitionSpec as P


AXES = ("xl", "c", "xh", "z", "y")
SIZES = (2, 2, 2, 8, 4)
EDGE = 8
REACH = 3
TAPS = 7
LANES = 128
PACK = 32


def shift(cells, axes, target):
    sizes = [SIZES[AXES.index(axis)] for axis in axes]
    pairs = []
    for place in np.ndindex(*sizes):
        goal = target(*place)
        if goal is not None:
            pairs.append((int(np.ravel_multi_index(place, sizes)), int(np.ravel_multi_index(goal, sizes))))
    return lax.ppermute(cells, axes if len(axes) > 1 else axes[0], pairs)


def swap_core(cells):
    return shift(cells, ("c",), lambda c: (1 - c,))


def side(cells):
    def target(xl, c, xh):
        x = (2 * xh + xl + (1 if c == 0 else 3)) % 4
        return (x % 2, c, x // 2)

    return shift(cells, ("xl", "c", "xh"), target)


def along_y(cells, step):
    return shift(cells, ("y",), lambda y: ((y + step) % 4,))


def neighbour(step):
    def target(xh, z, y):
        place = (xh * 8 + z) * 4 + y + step
        if not 0 <= place < 64:
            return None
        return (place // 32, place // 4 % 8, place % 4)

    return target


def added(*parts):
    total = parts[0].astype(jnp.float32)
    for part in parts[1:]:
        total = total + part.astype(jnp.float32)
    return total


def low_lanes(shape):
    return lax.broadcasted_iota(jnp.int32, shape, len(shape) - 1) < LANES // 2


def paired(cells):
    whole = cells + pltpu.roll(cells, LANES // 2, 1)
    head = whole.astype(jnp.bfloat16).astype(jnp.float32)
    return jnp.where(low_lanes(cells.shape), head, whole - head)


def thirds(cells):
    head = cells.astype(jnp.bfloat16)
    rest = cells - head.astype(jnp.float32)
    middle = rest.astype(jnp.bfloat16)
    return head, middle, (rest - middle.astype(jnp.float32)).astype(jnp.bfloat16)


def turning(size):
    place = lax.broadcasted_iota(jnp.int32, (size, size), 0) + lax.broadcasted_iota(jnp.int32, (size, size), 1)
    return (place == size - 1).astype(jnp.bfloat16)


def dot(a, b):
    return jnp.dot(a, b, preferred_element_type=jnp.float32)


def turned(cells, turn):
    size = turn.shape[0]
    count = cells.shape[1] // size
    return jnp.concatenate([dot(cells[:, at * size : (at + 1) * size], turn) for at in range(count)[::-1]], axis=1)


def edge_kernel(codes, last, first, up_last, up_first, table, before, after, looked):
    rows = codes.shape[1]
    features = table.shape[1]
    for start, cells, up, out in ((rows - EDGE, last, up_last, before), (0, first, up_first, after)):
        for at in range(EDGE):
            looked[at : at + 1] = table[pl.ds(codes[0, start + at], 1)]
        out[:, :features] = (cells[...].astype(jnp.float32) + looked[...]).astype(jnp.bfloat16)
        out[:, features:] = up[...]


def centre_kernel(
    place, codes, taps, window_far, table_far, up_far, stacks, columns, ups, taps_near, hot, window, table, up, done
):
    loads = [
        pltpu.make_async_copy(far, near, done.at[at])
        for at, (far, near) in enumerate(((window_far, window), (table_far, table), (up_far, up)))
    ]
    for load in loads:
        load.start()
    taps_near[...] = taps[...]
    rows, features = window.shape
    symbol = lax.broadcasted_iota(jnp.int32, (16, rows), 0)
    one_hot = jnp.where(symbol == codes[...], 1.0, 0.0).astype(jnp.bfloat16)
    for at in range(3):
        hot[:, at * rows : (at + 1) * rows] = one_hot
    width = features // 4
    turn = turning(256)
    by_row = jnp.broadcast_to(codes[...].astype(jnp.float32), (rows, rows)).T
    by_row = jnp.concatenate([by_row] * (width // rows), axis=1)
    for load in loads:
        load.wait()
    for r in range(4):
        cols = pl.ds(pl.multiple_of((place[0] ^ r) * width, width), width)
        looked = jnp.zeros((rows, width), jnp.float32)
        for symbol in range(table.shape[0]):
            looked = looked + jnp.where(by_row == symbol, table[symbol : symbol + 1, cols], 0.0)
        middle = (window[:, cols].astype(jnp.float32) + looked).astype(jnp.bfloat16)
        back = turned(middle, turn)
        stacks[r, :rows] = middle
        stacks[3 - r, rows:] = back.astype(jnp.bfloat16)
        columns[r, :, :rows] = middle.astype(jnp.float32).T.astype(jnp.bfloat16)
        columns[3 - r, :, rows:] = back.T.astype(jnp.bfloat16)
    ups[:rows] = up[...].astype(jnp.float32)
    ups[rows:] = turned(up[...], turn)


def early_kernel(place, centre, up_centre, before, after, w0, w1, stacks, ups, partial):
    rows = up_centre.shape[0] // 2
    features = 4 * centre.shape[2]
    width = centre.shape[2]
    total = rows + 2 * EDGE
    turn = turning(256)
    for r in range(4):
        cols = pl.ds(pl.multiple_of((place[0] ^ r) * width, width), width)
        halo = jnp.concatenate([before[:, cols].astype(jnp.float32), after[:, cols].astype(jnp.float32)], axis=0)
        halo = halo.astype(jnp.bfloat16)
        stacks[r, : 2 * rows] = centre[r]
        stacks[r, 2 * rows : 2 * rows + 2 * EDGE] = halo
        stacks[3 - r, 2 * rows + 2 * EDGE :] = turned(halo, turn).astype(jnp.bfloat16)
    for way in range(2):
        base = way * total
        ups[base + EDGE : base + EDGE + rows] = up_centre[way * rows : (way + 1) * rows]
        for part, start in ((before, base), (after, base + EDGE + rows)):
            cells = part[:, features:].astype(jnp.float32)
            if way == 1:
                cells = turned(cells.astype(jnp.bfloat16), turn)
            ups[start : start + EDGE] = cells
    add_products(partial, None, ((stacks.at[0], w0), (stacks.at[1], w1)))


def add_products(out, start, pairs):
    def step(at, _):
        cols = pl.ds(pl.multiple_of(at * 256, 256), 256)
        acc = added(*[dot(cells[...], w[:, cols]) for cells, w in pairs])
        if start is not None:
            acc = acc + start[:, cols]
        out[:, cols] = acc
        return 0

    lax.fori_loop(0, out.shape[1] // 256, step, 0)


def middle_kernel(stacks, partial, w, out, *, start):
    add_products(out, partial, ((stacks.at[2, :, start : start + w.shape[0]], w),))


def strand_kernel(stacks, partial, w3, w3_rest, ups, taps, grads, ahead, behind, sums, values, mixes, *, first):
    total = stacks.shape[1] // 2
    rows = total - 2 * EDGE
    units = sums.shape[1]
    split = w3.shape[0]
    count = units // LANES
    turn = turning(LANES)

    def project(at, _):
        near = pl.ds(pl.multiple_of(at * 256, 256), 256)
        cols = pl.ds(pl.multiple_of(first + at * 256, 256), 256)
        acc = partial[:, cols] + dot(stacks[3, :, :split], w3[:, cols]) + dot(stacks[3, :, split:], w3_rest[:, cols])
        acc = acc.astype(jnp.bfloat16).astype(jnp.float32)
        for way in range(2):
            base = way * total
            halo = 2 * rows + way * 2 * EDGE
            values[base : base + EDGE, near] = acc[halo : halo + EDGE]
            values[base + EDGE : base + EDGE + rows, near] = acc[way * rows : (way + 1) * rows]
            values[base + EDGE + rows : base + total, near] = acc[halo + EDGE : halo + 2 * EDGE]
        return 0

    lax.fori_loop(0, units // 256, project, 0)
    sums[...] = jnp.zeros(sums.shape, jnp.float32)

    def work(at, _):
        near = pl.ds(pl.multiple_of(at * LANES, LANES), LANES)
        cols = pl.ds(pl.multiple_of(first + at * LANES, LANES), LANES)
        for way in range(2):
            base = way * total
            places = [base + EDGE + (tap - REACH if way == 0 else REACH - tap) for tap in range(TAPS)]
            linear = values[base : base + total, near]
            logistic = jax.nn.sigmoid(linear)
            gating = linear * logistic
            up = ups[base : base + total, cols]
            grad_mix = up * gating
            mixes[way] = grad_mix
            mid = slice(EDGE, EDGE + rows)
            linear, logistic, gating, up, grad_mix = [
                cells[mid] for cells in (linear, logistic, gating, up, grad_mix)
            ]
            mixing = jnp.zeros((rows, LANES), jnp.float32)
            for tap in range(TAPS):
                moved = values[places[tap] : places[tap] + rows, near]
                mixing = mixing + taps[tap : tap + 1, cols] * moved
                sums[tap : tap + 1, near] += jnp.sum(grad_mix * moved, axis=0, keepdims=True)
            strand_out = mixing * gating
            acc = up * mixing * logistic * (1.0 + linear * (1.0 - logistic))
            for tap in range(TAPS):
                lower = 2 * EDGE - places[tap] + base
                acc = acc + taps[tap : tap + 1, cols] * mixes[way, lower : lower + rows]
            grads[way * rows : (way + 1) * rows, near] = acc.astype(jnp.bfloat16)
            if way == 0:
                ahead[:, near] = strand_out
            else:
                far = pl.ds(pl.multiple_of((count - 1 - at) * LANES, LANES), LANES)
                behind[:, far] = dot(strand_out.astype(jnp.bfloat16), turn)
        return 0

    lax.fori_loop(0, count, work, 0)


def product_kernel(columns, *refs, block):
    grads, out = refs[:-1], refs[-1]
    start = 0
    for part in grads:
        stop = start + part.shape[1]
        out[:, start:stop] = dot(columns[block], part[...]).astype(out.dtype)
        start = stop


def merge_kernel(columns, came, *refs, block):
    grads, out = refs[:-1], refs[-1]
    start = 0
    for part in grads:
        stop = start + part.shape[1]
        own = dot(columns[block], part[...])
        out[:, start:stop] = (own + came[:, start:stop].astype(jnp.float32)).astype(jnp.bfloat16)
        start = stop


def back_kernel(place, hot, w0, w1, w2, w2_rest, w3, w3_rest, later, *refs):
    parts, (out, block, packed, table, backs, grads, sums) = refs[:12], refs[12:]
    rows = out.shape[0]
    width = w0.shape[0]
    turn = turning(256)
    dims = (((1,), (1,)), ((), ()))
    start = 0
    for at in range(3):
        part, part_sums = parts[at * 4], parts[at * 4 + 3]
        stop = start + part.shape[1]
        grads[:, start:stop] = part[...]
        sums[:, start:stop] = part_sums[...]
        start = stop
    forward = jnp.concatenate([parts[at * 4 + 1][...] for at in range(3)], axis=1)
    backward = jnp.concatenate([parts[at * 4 + 2][...] for at in (2, 1, 0)], axis=1)
    block[...] = (forward + backward).astype(jnp.bfloat16)
    for r, group in enumerate(((w0,), (w1,), (w2, w2_rest), (w3, w3_rest))):
        size = width // len(group)
        for at, w in enumerate(group):
            backs[r, :, at * size : (at + 1) * size] = lax.dot_general(
                grads[...], w[...], dims, preferred_element_type=jnp.float32
            )
    for r in range(4):
        whole = backs[r, :rows] + turned(backs[3 - r, rows:].astype(jnp.bfloat16), turn)
        cols = pl.ds(pl.multiple_of((place[0] ^ r) * width, width), width)
        out[:, cols] = whole.astype(jnp.bfloat16)
        table[:, cols] = dot(hot[...], jnp.concatenate(thirds(whole), axis=0))
    count = sums.shape[1] // LANES
    half = table.shape[1] // 2
    for at in range(count):
        cols = slice(at * LANES, (at + 1) * LANES)
        packed[at * PACK : at * PACK + 8] = sums[:, cols]
        packed[at * PACK + 8 : at * PACK + 16] = table[:8, cols]
        packed[at * PACK + 16 : at * PACK + 24] = table[:8, half + at * LANES : half + (at + 1) * LANES]
        packed[at * PACK + 24 : at * PACK + 32] = jnp.zeros((8, LANES), jnp.float32)


def block_kernel(place, columns, mate, came, *refs, parts):
    grads, refs = refs[:parts], refs[parts:]
    wide = len(refs) > 5
    if wide:
        packed, packed_came, outs, own, extra = refs[0], refs[1], refs[2:6], refs[6], refs[7]
        whole = packed[...] + packed_came[...]
        half = whole.shape[0]
        head = whole.astype(jnp.bfloat16).astype(jnp.float32)
        rest = whole - head
        low = low_lanes(whole.shape)
        extra[:half] = jnp.where(low, head, pltpu.roll(rest, LANES // 2, 1))
        extra[half:] = jnp.where(low, pltpu.roll(head, LANES // 2, 1), rest)
    else:
        outs, own = refs[:4], refs[4]
    rows = outs[0].shape[0]
    units = own.shape[1]
    product_kernel(columns, *grads, own, block=0)
    for step, out in enumerate(outs):
        here = pl.ds(pl.multiple_of((place[1] + step) % 4 * rows, rows), rows)
        out[:, :units] = added(own[here], mate[here], came[here]).astype(jnp.bfloat16)
        if wide:
            out[:, units:] = extra[here].astype(jnp.bfloat16)


def quarter_kernel(*refs):
    head, tail, out = refs[:4], refs[4:8], refs[8]
    rows, units = head[0].shape
    size = 32

    def step(at, _):
        here = pl.ds(pl.multiple_of(at * size, size), size)
        out[here, :units] = added(*[part[here] for part in head]).astype(jnp.bfloat16)
        cells = added(*[part[here] for part in tail])
        out[here, units : 2 * units] = cells[:, :units].astype(jnp.bfloat16)
        out[here, 2 * units :] = paired(cells[:, units:]).astype(jnp.bfloat16)
        return 0

    lax.fori_loop(0, rows // size, step, 0)


def piece_kernel(parts, out):
    units = out.shape[2] - LANES
    total = parts[0].astype(jnp.float32)
    for at in range(1, parts.shape[0]):
        total = total + parts[at].astype(jnp.float32)
    plain = total[:, :units].astype(jnp.bfloat16)
    packed = paired(total[:, units:]).astype(jnp.bfloat16)
    for at in range(parts.shape[0]):
        out[at, :, :units] = plain
        out[at, :, units:] = packed


def final_kernel(place, q0, q1, q2, q3, weight_out, taps_out, table_out, packed, *, factor):
    rows = q0.shape[0]
    units = weight_out.shape[1]
    for step, part in enumerate((q0, q1, q2, q3)):
        there = pl.ds(pl.multiple_of((place[1] + 4 - step) % 4 * rows, rows), rows)
        weight_out[there] = part[:, :units].astype(jnp.float32) * factor
        packed[there] = part[:, units:].astype(jnp.float32)
    cells = packed[...]
    whole = cells + pltpu.roll(cells, LANES // 2, 1)
    half = whole.shape[0] // 2
    whole = jnp.where(low_lanes((half, LANES)), whole[:half], whole[half:]) * factor
    count = half // PACK
    symbols = table_out.shape[0]
    for at in range(count):
        cols = slice(at * LANES, (at + 1) * LANES)
        taps_out[:, cols] = whole[at * PACK : at * PACK + TAPS]
        table_out[:, cols] = whole[at * PACK + 8 : at * PACK + 8 + symbols]
        cols = slice(units + at * LANES, units + (at + 1) * LANES)
        table_out[:, cols] = whole[at * PACK + 16 : at * PACK + 16 + symbols]


def call(kernel, outs, *args, scratch=(), scalar=False, unread=(), **fixed):
    inside = pl.BlockSpec(memory_space=pltpu.VMEM)
    specs = [inside] * len(args)
    if scalar:
        specs[0] = pl.BlockSpec(memory_space=pltpu.SMEM)
    for at in unread:
        specs[at] = pl.BlockSpec(memory_space=pl.ANY)
    return pl.pallas_call(
        functools.partial(kernel, **fixed),
        out_shape=outs,
        in_specs=specs,
        out_specs=jax.tree.map(lambda _: inside, outs),
        scratch_shapes=list(scratch),
        compiler_params=pltpu.CompilerParams(vmem_limit_bytes=20 * 2**20),
    )(*args)


def array(shape, dtype=jnp.bfloat16):
    return jax.ShapeDtypeStruct(shape, dtype)


def step(hidden, tokens, embedding, weight, kernel, cotangent):
    window = hidden[0]
    upstream = cotangent[0]
    rows, features = window.shape
    units = weight.shape[1]
    symbols = embedding.shape[0]
    factor = 1.0 / math.sqrt(rows * 256)
    width = features // 4
    total = rows + 2 * EDGE
    me = 2 * lax.axis_index("xl") + lax.axis_index("c")
    place = jnp.stack([me, lax.axis_index("y")]).astype(jnp.int32)
    half = width // 2
    w_core = swap_core(weight)
    w_side = [side(weight[at * half : (at + 1) * half]) for at in range(2)]
    w_last = [swap_core(w_side[at]) for at in range(2)]
    top = pl.BlockSpec((EDGE, features), lambda at: (0, 0))
    bottom = pl.BlockSpec((EDGE, features), lambda at: (rows // EDGE - 1, 0))
    up_top = pl.BlockSpec((EDGE, units), lambda at: (0, 0))
    up_bottom = pl.BlockSpec((EDGE, units), lambda at: (rows // EDGE - 1, 0))
    edge = array((EDGE, features + units))
    before, after = pl.pallas_call(
        edge_kernel,
        out_shape=(edge, edge),
        grid=(1,),
        in_specs=[
            pl.BlockSpec(memory_space=pltpu.SMEM),
            bottom,
            top,
            up_bottom,
            up_top,
            pl.BlockSpec((symbols, features), lambda at: (0, 0)),
        ],
        out_specs=[pl.BlockSpec(edge.shape, lambda at: (0, 0))] * 2,
        scratch_shapes=[pltpu.VMEM((EDGE, features), jnp.float32)],
    )(tokens, window, window, upstream, upstream, embedding)
    before = shift(before, ("xh", "z", "y"), neighbour(1))
    after = shift(after, ("xh", "z", "y"), neighbour(-1))
    centre, columns, up_centre, taps, hot = call(
        centre_kernel,
        (
            array((4, 2 * rows, width)),
            array((4, width, 2 * rows)),
            array((2 * rows, units), jnp.float32),
            array(kernel.shape, jnp.float32),
            array((16, 3 * rows)),
        ),
        place,
        tokens,
        kernel,
        window,
        embedding,
        upstream,
        scalar=True,
        unread=(3, 4, 5),
        scratch=(
            pltpu.VMEM((rows, features), jnp.bfloat16),
            pltpu.VMEM((symbols, features), jnp.float32),
            pltpu.VMEM((rows, units), jnp.bfloat16),
            pltpu.SemaphoreType.DMA((3,)),
        ),
    )
    wide = array((2 * total, units), jnp.float32)
    stacks, ups, partial = call(
        early_kernel,
        (array((4, 2 * total, width)), wide, wide),
        place,
        centre,
        up_centre,
        before,
        after,
        weight,
        w_core,
        scalar=True,
    )
    for at in range(2):
        partial = call(middle_kernel, wide, stacks, partial, w_side[at], start=at * half)
    ends = (0, units // 2, units // 4 * 3, units)
    parts = []
    for at in range(3):
        size = ends[at + 1] - ends[at]
        parts.append(
            call(
                strand_kernel,
                (
                    array((2 * rows, size)),
                    array((rows, size), jnp.float32),
                    array((rows, size), jnp.float32),
                    array((8, size), jnp.float32),
                ),
                stacks,
                partial,
                *w_last,
                ups,
                taps,
                scratch=(pltpu.VMEM((2 * total, size), jnp.float32), pltpu.VMEM((2, total, LANES), jnp.float32)),
                first=ends[at],
            )
        )
    grads = [[parts[0][0]], [parts[1][0], parts[2][0]]]
    chunk = array((width, units // 2))
    came = []
    mates = []
    for at in range(2):
        goes = call(product_kernel, chunk, columns, *grads[at], block=3)
        goes = swap_core(goes)
        merged = call(merge_kernel, chunk, columns, goes, *grads[at], block=2)
        came.append(side(merged))
        mate = call(product_kernel, chunk, columns, *grads[at], block=1)
        mates.append(swap_core(mate))
    grad_hidden, block_result, packed = call(
        back_kernel,
        (
            array((rows, features)),
            array((rows, units)),
            array((units // LANES * PACK, LANES), jnp.float32),
        ),
        place,
        hot,
        weight,
        w_core,
        *w_side,
        *w_last,
        merged,
        *[cells for part in parts for cells in part],
        scalar=True,
        unread=(8,),
        scratch=(
            pltpu.VMEM((16, features), jnp.float32),
            pltpu.VMEM((4, 2 * rows, width), jnp.float32),
            pltpu.VMEM((2 * rows, units), jnp.bfloat16),
            pltpu.VMEM((8, units), jnp.float32),
        ),
    )
    packed = packed + swap_core(packed)
    packed_came = side(packed)
    part = width // 4
    own = pltpu.VMEM(chunk.shape, jnp.float32)
    head = call(
        block_kernel,
        (array((part, units // 2)),) * 4,
        place,
        columns,
        mates[0],
        came[0],
        *grads[0],
        scalar=True,
        scratch=(own,),
        parts=1,
    )
    head = [head[0]] + [along_y(head[step], step) for step in (1, 2, 3)]
    tail = call(
        block_kernel,
        (array((part, units // 2 + LANES)),) * 4,
        place,
        columns,
        mates[1],
        came[1],
        *grads[1],
        packed,
        packed_came,
        scalar=True,
        scratch=(own, pltpu.VMEM((width, LANES), jnp.float32)),
        parts=2,
    )
    tail = [tail[0]] + [along_y(tail[step], step) for step in (1, 2, 3)]
    quarter = call(quarter_kernel, array((part, units + LANES)), *head, *tail)
    pieces = quarter.reshape(16, part // 16, -1)
    pieces = lax.all_to_all(pieces, ("xh", "z"), split_axis=0, concat_axis=0, tiled=True)
    pieces = call(piece_kernel, array(pieces.shape), pieces)
    pieces = lax.all_to_all(pieces, ("xh", "z"), split_axis=0, concat_axis=0, tiled=True)
    quarter = pieces.reshape(quarter.shape)
    quarters = [quarter] + [along_y(quarter, step) for step in (1, 2, 3)]
    grad_weight, grad_kernel, grad_embedding = call(
        final_kernel,
        (array((width, units), jnp.float32), array(kernel.shape, jnp.float32), array(embedding.shape, jnp.float32)),
        place,
        *quarters,
        scalar=True,
        scratch=(pltpu.VMEM((width, LANES), jnp.float32),),
        factor=factor,
    )
    return block_result[None], grad_hidden[None], grad_weight, grad_kernel, grad_embedding


def solution(mesh):
    fine = Mesh(mesh.devices.reshape(SIZES), AXES)
    batch = ("xl", "c")
    spot = ("xh", "z", "y")
    in_specs = (P(batch, spot, None), P(batch, spot), P(), P(batch, None), P(), P(batch, spot, None))
    out_specs = (P(batch, spot, None), P(batch, spot, None), P(batch, None), P(), P())
    return jax.shard_map(step, mesh=fine, in_specs=in_specs, out_specs=out_specs, check_vma=False)
```

```python
import functools
import math

import jax
import jax.numpy as jnp
import numpy as np
from jax import lax
from jax.experimental import pallas as pl
from jax.experimental.pallas import tpu as pltpu
from jax.sharding import Mesh, PartitionSpec as P


AXES = ("xl", "c", "xh", "z", "y")
SIZES = (2, 2, 2, 8, 4)
EDGE = 8
REACH = 3
TAPS = 7
LANES = 128
PACK = 32


def shift(cells, axes, target):
    sizes = [SIZES[AXES.index(axis)] for axis in axes]
    pairs = []
    for place in np.ndindex(*sizes):
        goal = target(*place)
        if goal is not None:
            pairs.append((int(np.ravel_multi_index(place, sizes)), int(np.ravel_multi_index(goal, sizes))))
    return lax.ppermute(cells, axes if len(axes) > 1 else axes[0], pairs)


def swap_core(cells):
    return shift(cells, ("c",), lambda c: (1 - c,))


def side(cells):
    def target(xl, c, xh):
        x = (2 * xh + xl + (1 if c == 0 else 3)) % 4
        return (x % 2, c, x // 2)

    return shift(cells, ("xl", "c", "xh"), target)


def along_y(cells, step):
    return shift(cells, ("y",), lambda y: ((y + step) % 4,))


def neighbour(step):
    def target(xh, z, y):
        place = (xh * 8 + z) * 4 + y + step
        if not 0 <= place < 64:
            return None
        return (place // 32, place // 4 % 8, place % 4)

    return target


def added(*parts):
    total = parts[0].astype(jnp.float32)
    for part in parts[1:]:
        total = total + part.astype(jnp.float32)
    return total


def low_lanes(shape):
    return lax.broadcasted_iota(jnp.int32, shape, len(shape) - 1) < LANES // 2


def paired(cells):
    whole = cells + pltpu.roll(cells, LANES // 2, 1)
    head = whole.astype(jnp.bfloat16).astype(jnp.float32)
    return jnp.where(low_lanes(cells.shape), head, whole - head)


def thirds(cells):
    head = cells.astype(jnp.bfloat16)
    rest = cells - head.astype(jnp.float32)
    middle = rest.astype(jnp.bfloat16)
    return head, middle, (rest - middle.astype(jnp.float32)).astype(jnp.bfloat16)


def turning(size):
    place = lax.broadcasted_iota(jnp.int32, (size, size), 0) + lax.broadcasted_iota(jnp.int32, (size, size), 1)
    return (place == size - 1).astype(jnp.bfloat16)


def dot(a, b):
    return jnp.dot(a, b, preferred_element_type=jnp.float32)


def turned(cells, turn):
    size = turn.shape[0]
    count = cells.shape[1] // size
    return jnp.concatenate([dot(cells[:, at * size : (at + 1) * size], turn) for at in range(count)[::-1]], axis=1)


def edge_kernel(codes, last, first, up_last, up_first, table, before, after, looked):
    rows = codes.shape[1]
    features = table.shape[1]
    for start, cells, up, out in ((rows - EDGE, last, up_last, before), (0, first, up_first, after)):
        for at in range(EDGE):
            looked[at : at + 1] = table[pl.ds(codes[0, start + at], 1)]
        out[:, :features] = (cells[...].astype(jnp.float32) + looked[...]).astype(jnp.bfloat16)
        out[:, features:] = up[...]


def centre_kernel(
    place, codes, taps, window_far, table_far, up_far, stacks, columns, ups, taps_near, hot, window, table, up, done
):
    loads = [
        pltpu.make_async_copy(far, near, done.at[at])
        for at, (far, near) in enumerate(((window_far, window), (table_far, table), (up_far, up)))
    ]
    for load in loads:
        load.start()
    taps_near[...] = taps[...]
    rows, features = window.shape
    symbol = lax.broadcasted_iota(jnp.int32, (16, rows), 0)
    one_hot = jnp.where(symbol == codes[...], 1.0, 0.0).astype(jnp.bfloat16)
    for at in range(3):
        hot[:, at * rows : (at + 1) * rows] = one_hot
    width = features // 4
    turn = turning(256)
    by_row = jnp.broadcast_to(codes[...].astype(jnp.float32), (rows, rows)).T
    by_row = jnp.concatenate([by_row] * (width // rows), axis=1)
    for load in loads:
        load.wait()
    for r in range(4):
        cols = pl.ds(pl.multiple_of((place[0] ^ r) * width, width), width)
        looked = jnp.zeros((rows, width), jnp.float32)
        for symbol in range(table.shape[0]):
            looked = looked + jnp.where(by_row == symbol, table[symbol : symbol + 1, cols], 0.0)
        middle = (window[:, cols].astype(jnp.float32) + looked).astype(jnp.bfloat16)
        back = turned(middle, turn)
        stacks[r, :rows] = middle
        stacks[3 - r, rows:] = back.astype(jnp.bfloat16)
        columns[r, :, :rows] = middle.astype(jnp.float32).T.astype(jnp.bfloat16)
        columns[3 - r, :, rows:] = back.T.astype(jnp.bfloat16)
    ups[:rows] = up[...].astype(jnp.float32)
    ups[rows:] = turned(up[...], turn)


def early_kernel(place, centre, up_centre, before, after, w0, w1, stacks, ups, partial):
    rows = up_centre.shape[0] // 2
    features = 4 * centre.shape[2]
    width = centre.shape[2]
    total = rows + 2 * EDGE
    turn = turning(256)
    for r in range(4):
        cols = pl.ds(pl.multiple_of((place[0] ^ r) * width, width), width)
        halo = jnp.concatenate([before[:, cols].astype(jnp.float32), after[:, cols].astype(jnp.float32)], axis=0)
        halo = halo.astype(jnp.bfloat16)
        stacks[r, : 2 * rows] = centre[r]
        stacks[r, 2 * rows : 2 * rows + 2 * EDGE] = halo
        stacks[3 - r, 2 * rows + 2 * EDGE :] = turned(halo, turn).astype(jnp.bfloat16)
    for way in range(2):
        base = way * total
        ups[base + EDGE : base + EDGE + rows] = up_centre[way * rows : (way + 1) * rows]
        for part, start in ((before, base), (after, base + EDGE + rows)):
            cells = part[:, features:].astype(jnp.float32)
            if way == 1:
                cells = turned(cells.astype(jnp.bfloat16), turn)
            ups[start : start + EDGE] = cells
    add_products(partial, None, ((stacks.at[0], w0), (stacks.at[1], w1)))


def add_products(out, start, pairs):
    def step(at, _):
        cols = pl.ds(pl.multiple_of(at * 256, 256), 256)
        acc = added(*[dot(cells[...], w[:, cols]) for cells, w in pairs])
        if start is not None:
            acc = acc + start[:, cols]
        out[:, cols] = acc
        return 0

    lax.fori_loop(0, out.shape[1] // 256, step, 0)


def middle_kernel(stacks, partial, w2, out):
    add_products(out, partial, ((stacks.at[2], w2),))


def strand_kernel(stacks, partial, w3, ups, taps, grads, ahead, behind, sums, values, mixes, *, first):
    total = stacks.shape[1] // 2
    rows = total - 2 * EDGE
    units = sums.shape[1]
    count = units // LANES
    turn = turning(LANES)

    def project(at, _):
        near = pl.ds(pl.multiple_of(at * 256, 256), 256)
        cols = pl.ds(pl.multiple_of(first + at * 256, 256), 256)
        acc = partial[:, cols] + dot(stacks[3], w3[:, cols])
        acc = acc.astype(jnp.bfloat16).astype(jnp.float32)
        for way in range(2):
            base = way * total
            halo = 2 * rows + way * 2 * EDGE
            values[base : base + EDGE, near] = acc[halo : halo + EDGE]
            values[base + EDGE : base + EDGE + rows, near] = acc[way * rows : (way + 1) * rows]
            values[base + EDGE + rows : base + total, near] = acc[halo + EDGE : halo + 2 * EDGE]
        return 0

    lax.fori_loop(0, units // 256, project, 0)
    sums[...] = jnp.zeros(sums.shape, jnp.float32)

    def work(at, _):
        near = pl.ds(pl.multiple_of(at * LANES, LANES), LANES)
        cols = pl.ds(pl.multiple_of(first + at * LANES, LANES), LANES)
        for way in range(2):
            base = way * total
            places = [base + EDGE + (tap - REACH if way == 0 else REACH - tap) for tap in range(TAPS)]
            linear = values[base : base + total, near]
            logistic = jax.nn.sigmoid(linear)
            gating = linear * logistic
            up = ups[base : base + total, cols]
            grad_mix = up * gating
            mixes[way] = grad_mix
            mid = slice(EDGE, EDGE + rows)
            linear, logistic, gating, up, grad_mix = [
                cells[mid] for cells in (linear, logistic, gating, up, grad_mix)
            ]
            mixing = jnp.zeros((rows, LANES), jnp.float32)
            for tap in range(TAPS):
                moved = values[places[tap] : places[tap] + rows, near]
                mixing = mixing + taps[tap : tap + 1, cols] * moved
                sums[tap : tap + 1, near] += jnp.sum(grad_mix * moved, axis=0, keepdims=True)
            strand_out = mixing * gating
            acc = up * mixing * logistic * (1.0 + linear * (1.0 - logistic))
            for tap in range(TAPS):
                lower = 2 * EDGE - places[tap] + base
                acc = acc + taps[tap : tap + 1, cols] * mixes[way, lower : lower + rows]
            grads[way * rows : (way + 1) * rows, near] = acc.astype(jnp.bfloat16)
            if way == 0:
                ahead[:, near] = strand_out
            else:
                far = pl.ds(pl.multiple_of((count - 1 - at) * LANES, LANES), LANES)
                behind[:, far] = dot(strand_out.astype(jnp.bfloat16), turn)
        return 0

    lax.fori_loop(0, count, work, 0)


def product_kernel(columns, *refs, block, parts):
    grads, refs = refs[:parts], refs[parts:]
    out = refs[-1]
    start = 0
    for part in grads:
        stop = start + part.shape[1]
        out[:, start:stop] = dot(columns[block], part[...]).astype(out.dtype)
        start = stop
    if len(refs) > 1:
        out[:, start:] = refs[0][...]


def merge_kernel(columns, came, *refs, block, parts):
    grads, refs = refs[:parts], refs[parts:]
    out = refs[-1]
    start = 0
    for part in grads:
        stop = start + part.shape[1]
        own = dot(columns[block], part[...])
        out[:, start:stop] = (own + came[:, start:stop].astype(jnp.float32)).astype(jnp.bfloat16)
        start = stop
    if len(refs) > 1:
        out[:, start:] = paired(added(refs[0][...], came[:, start:])).astype(jnp.bfloat16)


def small_kernel(place, hot, w0, w1, w2, w3, *refs):
    parts, (out, grads, sums, table) = refs[:6], refs[6:]
    rows = hot.shape[1] // 3
    start = 0
    for at in range(3):
        part, part_sums = parts[at * 2], parts[at * 2 + 1]
        stop = start + part.shape[1]
        grads[:8, start:stop] = dot(hot[:, :rows], part[:rows])[:8]
        grads[8:, start:stop] = dot(hot[:, :rows], part[rows:])[:8]
        sums[:, start:stop] = part_sums[...]
        start = stop
    split = jnp.concatenate(thirds(grads[...]), axis=0)
    turn = turning(256)
    width = w0.shape[0]
    dims = (((1,), (1,)), ((), ()))
    backs = []
    for w in (w0, w1, w2, w3):
        back = lax.dot_general(split, w[...], dims, preferred_element_type=jnp.float32)
        backs.append(back[:16] + back[16:32] + back[32:])
    for r in range(4):
        cols = pl.ds(pl.multiple_of((place[0] ^ r) * width, width), width)
        there = turned(jnp.concatenate(thirds(backs[3 - r][8:]), axis=0), turn)
        table[:, cols] = backs[r][:8] + there[:8] + there[8:16] + there[16:]
    units = sums.shape[1]
    count = units // LANES
    for at in range(count):
        pack = jnp.concatenate(
            [
                sums[:, at * LANES : (at + 1) * LANES],
                table[:, at * LANES : (at + 1) * LANES],
                table[:, units + at * LANES : units + (at + 1) * LANES],
                jnp.zeros((8, LANES), jnp.float32),
            ],
            axis=0,
        )
        head = pack.astype(jnp.bfloat16).astype(jnp.float32)
        rest = pack - head
        low = low_lanes(pack.shape)
        first = jnp.where(low, head, pltpu.roll(rest, LANES // 2, 1))
        second = jnp.where(low, pltpu.roll(head, LANES // 2, 1), rest)
        out[at * PACK : (at + 1) * PACK] = first.astype(jnp.bfloat16)
        out[(count + at) * PACK : (count + at + 1) * PACK] = second.astype(jnp.bfloat16)


def back_kernel(place, w0, w1, w2, w3, later, *refs):
    parts, (out, block, backs, grads) = refs[:9], refs[9:]
    rows = out.shape[0]
    width = w0.shape[0]
    turn = turning(256)
    dims = (((1,), (1,)), ((), ()))
    start = 0
    for at in range(3):
        part = parts[at * 3]
        stop = start + part.shape[1]
        grads[:, start:stop] = part[...]
        start = stop
    forward = jnp.concatenate([parts[at * 3 + 1][...] for at in range(3)], axis=1)
    backward = jnp.concatenate([parts[at * 3 + 2][...] for at in (2, 1, 0)], axis=1)
    block[...] = (forward + backward).astype(jnp.bfloat16)
    for r, w in enumerate((w0, w1, w2, w3)):
        backs[r] = lax.dot_general(grads[...], w[...], dims, preferred_element_type=jnp.float32)
    for r in range(4):
        whole = backs[r, :rows] + turned(backs[3 - r, rows:].astype(jnp.bfloat16), turn)
        out[:, pl.ds(pl.multiple_of((place[0] ^ r) * width, width), width)] = whole.astype(jnp.bfloat16)


def block_kernel(place, columns, mate, came, *refs, parts):
    grads, refs = refs[:parts], refs[parts:]
    wide = len(refs) > 5
    if wide:
        merged, outs, own, extra = refs[0], refs[1:5], refs[5], refs[6]
        extra[...] = paired(added(merged[:, own.shape[1] :], came[:, own.shape[1] :]))
    else:
        outs, own = refs[:4], refs[4]
    rows = outs[0].shape[0]
    units = own.shape[1]
    product_kernel(columns, *grads, own, block=0, parts=parts)
    for step, out in enumerate(outs):
        here = pl.ds(pl.multiple_of((place[1] + step) % 4 * rows, rows), rows)
        out[:, :units] = added(own[here], mate[here], came[here, :units]).astype(jnp.bfloat16)
        if wide:
            out[:, units:] = extra[here].astype(jnp.bfloat16)


def quarter_kernel(*refs):
    head, tail, out = refs[:4], refs[4:8], refs[8]
    rows, units = head[0].shape
    size = 32

    def step(at, _):
        here = pl.ds(pl.multiple_of(at * size, size), size)
        out[here, :units] = added(*[part[here] for part in head]).astype(jnp.bfloat16)
        cells = added(*[part[here] for part in tail])
        out[here, units : 2 * units] = cells[:, :units].astype(jnp.bfloat16)
        out[here, 2 * units :] = paired(cells[:, units:]).astype(jnp.bfloat16)
        return 0

    lax.fori_loop(0, rows // size, step, 0)


def piece_kernel(parts, out):
    units = out.shape[2] - LANES
    total = parts[0].astype(jnp.float32)
    for at in range(1, parts.shape[0]):
        total = total + parts[at].astype(jnp.float32)
    plain = total[:, :units].astype(jnp.bfloat16)
    packed = paired(total[:, units:]).astype(jnp.bfloat16)
    for at in range(parts.shape[0]):
        out[at, :, :units] = plain
        out[at, :, units:] = packed


def final_kernel(place, q0, q1, q2, q3, weight_out, taps_out, table_out, packed, *, factor):
    rows = q0.shape[0]
    units = weight_out.shape[1]
    for step, part in enumerate((q0, q1, q2, q3)):
        there = pl.ds(pl.multiple_of((place[1] + 4 - step) % 4 * rows, rows), rows)
        weight_out[there] = part[:, :units].astype(jnp.float32) * factor
        packed[there] = part[:, units:].astype(jnp.float32)
    cells = packed[...]
    whole = cells + pltpu.roll(cells, LANES // 2, 1)
    half = whole.shape[0] // 2
    whole = jnp.where(low_lanes((half, LANES)), whole[:half], whole[half:]) * factor
    count = half // PACK
    symbols = table_out.shape[0]
    for at in range(count):
        cols = slice(at * LANES, (at + 1) * LANES)
        taps_out[:, cols] = whole[at * PACK : at * PACK + TAPS]
        table_out[:, cols] = whole[at * PACK + 8 : at * PACK + 8 + symbols]
        cols = slice(units + at * LANES, units + (at + 1) * LANES)
        table_out[:, cols] = whole[at * PACK + 16 : at * PACK + 16 + symbols]


def call(kernel, outs, *args, scratch=(), scalar=False, unread=(), **fixed):
    inside = pl.BlockSpec(memory_space=pltpu.VMEM)
    specs = [inside] * len(args)
    if scalar:
        specs[0] = pl.BlockSpec(memory_space=pltpu.SMEM)
    for at in unread:
        specs[at] = pl.BlockSpec(memory_space=pl.ANY)
    return pl.pallas_call(
        functools.partial(kernel, **fixed),
        out_shape=outs,
        in_specs=specs,
        out_specs=jax.tree.map(lambda _: inside, outs),
        scratch_shapes=list(scratch),
        compiler_params=pltpu.CompilerParams(vmem_limit_bytes=20 * 2**20),
    )(*args)


def array(shape, dtype=jnp.bfloat16):
    return jax.ShapeDtypeStruct(shape, dtype)


def step(hidden, tokens, embedding, weight, kernel, cotangent):
    window = hidden[0]
    upstream = cotangent[0]
    rows, features = window.shape
    units = weight.shape[1]
    symbols = embedding.shape[0]
    factor = 1.0 / math.sqrt(rows * 256)
    width = features // 4
    total = rows + 2 * EDGE
    me = 2 * lax.axis_index("xl") + lax.axis_index("c")
    place = jnp.stack([me, lax.axis_index("y")]).astype(jnp.int32)
    weights = [weight, swap_core(weight), side(weight)]
    weights.append(swap_core(weights[2]))
    top = pl.BlockSpec((EDGE, features), lambda at: (0, 0))
    bottom = pl.BlockSpec((EDGE, features), lambda at: (rows // EDGE - 1, 0))
    up_top = pl.BlockSpec((EDGE, units), lambda at: (0, 0))
    up_bottom = pl.BlockSpec((EDGE, units), lambda at: (rows // EDGE - 1, 0))
    edge = array((EDGE, features + units))
    before, after = pl.pallas_call(
        edge_kernel,
        out_shape=(edge, edge),
        grid=(1,),
        in_specs=[
            pl.BlockSpec(memory_space=pltpu.SMEM),
            bottom,
            top,
            up_bottom,
            up_top,
            pl.BlockSpec((symbols, features), lambda at: (0, 0)),
        ],
        out_specs=[pl.BlockSpec(edge.shape, lambda at: (0, 0))] * 2,
        scratch_shapes=[pltpu.VMEM((EDGE, features), jnp.float32)],
    )(tokens, window, window, upstream, upstream, embedding)
    before = shift(before, ("xh", "z", "y"), neighbour(1))
    after = shift(after, ("xh", "z", "y"), neighbour(-1))
    centre, columns, up_centre, taps, hot = call(
        centre_kernel,
        (
            array((4, 2 * rows, width)),
            array((4, width, 2 * rows)),
            array((2 * rows, units), jnp.float32),
            array(kernel.shape, jnp.float32),
            array((16, 3 * rows)),
        ),
        place,
        tokens,
        kernel,
        window,
        embedding,
        upstream,
        scalar=True,
        unread=(3, 4, 5),
        scratch=(
            pltpu.VMEM((rows, features), jnp.bfloat16),
            pltpu.VMEM((symbols, features), jnp.float32),
            pltpu.VMEM((rows, units), jnp.bfloat16),
            pltpu.SemaphoreType.DMA((3,)),
        ),
    )
    wide = array((2 * total, units), jnp.float32)
    stacks, ups, partial = call(
        early_kernel,
        (array((4, 2 * total, width)), wide, wide),
        place,
        centre,
        up_centre,
        before,
        after,
        *weights[:2],
        scalar=True,
    )
    partial = call(middle_kernel, wide, stacks, partial, weights[2])
    ends = (0, units // 2, units // 4 * 3, units)
    parts = []
    for at in range(3):
        size = ends[at + 1] - ends[at]
        parts.append(
            call(
                strand_kernel,
                (
                    array((2 * rows, size)),
                    array((rows, size), jnp.float32),
                    array((rows, size), jnp.float32),
                    array((8, size), jnp.float32),
                ),
                stacks,
                partial,
                weights[3],
                ups,
                taps,
                scratch=(pltpu.VMEM((2 * total, size), jnp.float32), pltpu.VMEM((2, total, LANES), jnp.float32)),
                first=ends[at],
            )
        )
    grads = [[parts[0][0]], [parts[1][0], parts[2][0]]]
    extra = call(
        small_kernel,
        array((width, LANES)),
        place,
        hot,
        *weights,
        *[cells for part in parts for cells in (part[0], part[3])],
        scalar=True,
        scratch=(
            pltpu.VMEM((16, units), jnp.float32),
            pltpu.VMEM((8, units), jnp.float32),
            pltpu.VMEM((8, features), jnp.float32),
        ),
    )
    chunk = array((width, units // 2))
    came = []
    mates = []
    for at in range(2):
        count = len(grads[at])
        rest = [extra] * at
        large = array((width, units // 2 + LANES * at))
        goes = call(product_kernel, large, columns, *grads[at], *rest, block=3, parts=count)
        goes = swap_core(goes)
        merged = call(merge_kernel, large, columns, goes, *grads[at], *rest, block=2, parts=count)
        came.append(side(merged))
        mate = call(product_kernel, chunk, columns, *grads[at], block=1, parts=count)
        mates.append(swap_core(mate))
    part = width // 4
    own = pltpu.VMEM(chunk.shape, jnp.float32)
    head = call(
        block_kernel,
        (array((part, units // 2)),) * 4,
        place,
        columns,
        mates[0],
        came[0],
        *grads[0],
        scalar=True,
        scratch=(own,),
        parts=1,
    )
    head = [head[0]] + [along_y(head[step], step) for step in (1, 2, 3)]
    tail = call(
        block_kernel,
        (array((part, units // 2 + LANES)),) * 4,
        place,
        columns,
        mates[1],
        came[1],
        *grads[1],
        merged,
        scalar=True,
        scratch=(own, pltpu.VMEM((width, LANES), jnp.float32)),
        parts=2,
    )
    grad_hidden, block_result = call(
        back_kernel,
        (array((rows, features)), array((rows, units))),
        place,
        *weights,
        tail[0],
        *[cells for part in parts for cells in part[:3]],
        scalar=True,
        unread=(5,),
        scratch=(pltpu.VMEM((4, 2 * rows, width), jnp.float32), pltpu.VMEM((2 * rows, units), jnp.bfloat16)),
    )
    tail = [tail[0]] + [along_y(tail[step], step) for step in (1, 2, 3)]
    quarter = call(quarter_kernel, array((part, units + LANES)), *head, *tail)
    pieces = quarter.reshape(16, part // 16, -1)
    pieces = lax.all_to_all(pieces, ("xh", "z"), split_axis=0, concat_axis=0, tiled=True)
    pieces = call(piece_kernel, array(pieces.shape), pieces)
    pieces = lax.all_to_all(pieces, ("xh", "z"), split_axis=0, concat_axis=0, tiled=True)
    quarter = pieces.reshape(quarter.shape)
    quarters = [quarter] + [along_y(quarter, step) for step in (1, 2, 3)]
    grad_weight, grad_kernel, grad_embedding = call(
        final_kernel,
        (array((width, units), jnp.float32), array(kernel.shape, jnp.float32), array(embedding.shape, jnp.float32)),
        place,
        *quarters,
        scalar=True,
        scratch=(pltpu.VMEM((width, LANES), jnp.float32),),
        factor=factor,
    )
    return block_result[None], grad_hidden[None], grad_weight, grad_kernel, grad_embedding


def solution(mesh):
    fine = Mesh(mesh.devices.reshape(SIZES), AXES)
    batch = ("xl", "c")
    spot = ("xh", "z", "y")
    in_specs = (P(batch, spot, None), P(batch, spot), P(), P(batch, None), P(), P(batch, spot, None))
    out_specs = (P(batch, spot, None), P(batch, spot, None), P(batch, None), P(), P())
    return jax.shard_map(step, mesh=fine, in_specs=in_specs, out_specs=out_specs, check_vma=False)
```

```python
import functools
import math

import jax
import jax.numpy as jnp
import numpy as np
from jax import lax
from jax.experimental import pallas as pl
from jax.experimental.pallas import tpu as pltpu
from jax.sharding import Mesh, PartitionSpec as P


AXES = ("xl", "c", "xh", "z", "y")
SIZES = (2, 2, 2, 8, 4)
EDGE = 8
REACH = 3
TAPS = 7
LANES = 128
PACK = 32


def shift(cells, axes, target):
    sizes = [SIZES[AXES.index(axis)] for axis in axes]
    pairs = []
    for place in np.ndindex(*sizes):
        goal = target(*place)
        if goal is not None:
            pairs.append((int(np.ravel_multi_index(place, sizes)), int(np.ravel_multi_index(goal, sizes))))
    return lax.ppermute(cells, axes if len(axes) > 1 else axes[0], pairs)


def swap_core(cells):
    return shift(cells, ("c",), lambda c: (1 - c,))


def side(cells):
    def target(xl, c, xh):
        x = (2 * xh + xl + (1 if c == 0 else 3)) % 4
        return (x % 2, c, x // 2)

    return shift(cells, ("xl", "c", "xh"), target)


def along_y(cells, step):
    return shift(cells, ("y",), lambda y: ((y + step) % 4,))


def neighbour(step):
    def target(xh, z, y):
        place = (xh * 8 + z) * 4 + y + step
        if not 0 <= place < 64:
            return None
        return (place // 32, place // 4 % 8, place % 4)

    return target


def added(*parts):
    total = parts[0].astype(jnp.float32)
    for part in parts[1:]:
        total = total + part.astype(jnp.float32)
    return total


def low_lanes(shape):
    return lax.broadcasted_iota(jnp.int32, shape, len(shape) - 1) < LANES // 2


def paired(cells):
    whole = cells + pltpu.roll(cells, LANES // 2, 1)
    head = whole.astype(jnp.bfloat16).astype(jnp.float32)
    return jnp.where(low_lanes(cells.shape), head, whole - head)


def thirds(cells):
    head = cells.astype(jnp.bfloat16)
    rest = cells - head.astype(jnp.float32)
    middle = rest.astype(jnp.bfloat16)
    return head, middle, (rest - middle.astype(jnp.float32)).astype(jnp.bfloat16)


def turning(size):
    place = lax.broadcasted_iota(jnp.int32, (size, size), 0) + lax.broadcasted_iota(jnp.int32, (size, size), 1)
    return (place == size - 1).astype(jnp.bfloat16)


def dot(a, b):
    return jnp.dot(a, b, preferred_element_type=jnp.float32)


def turned(cells, turn):
    size = turn.shape[0]
    count = cells.shape[1] // size
    return jnp.concatenate([dot(cells[:, at * size : (at + 1) * size], turn) for at in range(count)[::-1]], axis=1)


def edge_kernel(codes, last, first, up_last, up_first, table, before, after, looked):
    rows = codes.shape[1]
    features = table.shape[1]
    for start, cells, up, out in ((rows - EDGE, last, up_last, before), (0, first, up_first, after)):
        for at in range(EDGE):
            looked[at : at + 1] = table[pl.ds(codes[0, start + at], 1)]
        out[:, :features] = (cells[...].astype(jnp.float32) + looked[...]).astype(jnp.bfloat16)
        out[:, features:] = up[...]


def centre_kernel(
    place, codes, taps, window_far, table_far, up_far, stacks, columns, ups, taps_near, hot, window, table, up, done
):
    loads = [
        pltpu.make_async_copy(far, near, done.at[at])
        for at, (far, near) in enumerate(((window_far, window), (table_far, table), (up_far, up)))
    ]
    for load in loads:
        load.start()
    taps_near[...] = taps[...]
    rows, features = window.shape
    symbol = lax.broadcasted_iota(jnp.int32, (16, rows), 0)
    one_hot = jnp.where(symbol == codes[...], 1.0, 0.0).astype(jnp.bfloat16)
    for at in range(3):
        hot[:, at * rows : (at + 1) * rows] = one_hot
    width = features // 4
    turn = turning(256)
    by_row = jnp.broadcast_to(codes[...].astype(jnp.float32), (rows, rows)).T
    by_row = jnp.concatenate([by_row] * (width // rows), axis=1)
    for load in loads:
        load.wait()
    for r in range(4):
        cols = pl.ds(pl.multiple_of((place[0] ^ r) * width, width), width)
        looked = jnp.zeros((rows, width), jnp.float32)
        for symbol in range(table.shape[0]):
            looked = looked + jnp.where(by_row == symbol, table[symbol : symbol + 1, cols], 0.0)
        middle = (window[:, cols].astype(jnp.float32) + looked).astype(jnp.bfloat16)
        back = turned(middle, turn)
        stacks[r, :rows] = middle
        stacks[3 - r, rows:] = back.astype(jnp.bfloat16)
        columns[r, :, :rows] = middle.astype(jnp.float32).T.astype(jnp.bfloat16)
        columns[3 - r, :, rows:] = back.T.astype(jnp.bfloat16)
    ups[:rows] = up[...].astype(jnp.float32)
    ups[rows:] = turned(up[...], turn)


def early_kernel(place, centre, up_centre, before, after, w0, w1, stacks, ups, partial):
    rows = up_centre.shape[0] // 2
    features = 4 * centre.shape[2]
    width = centre.shape[2]
    total = rows + 2 * EDGE
    turn = turning(256)
    for r in range(4):
        cols = pl.ds(pl.multiple_of((place[0] ^ r) * width, width), width)
        halo = jnp.concatenate([before[:, cols].astype(jnp.float32), after[:, cols].astype(jnp.float32)], axis=0)
        halo = halo.astype(jnp.bfloat16)
        stacks[r, : 2 * rows] = centre[r]
        stacks[r, 2 * rows : 2 * rows + 2 * EDGE] = halo
        stacks[3 - r, 2 * rows + 2 * EDGE :] = turned(halo, turn).astype(jnp.bfloat16)
    for way in range(2):
        base = way * total
        ups[base + EDGE : base + EDGE + rows] = up_centre[way * rows : (way + 1) * rows]
        for part, start in ((before, base), (after, base + EDGE + rows)):
            cells = part[:, features:].astype(jnp.float32)
            if way == 1:
                cells = turned(cells.astype(jnp.bfloat16), turn)
            ups[start : start + EDGE] = cells
    add_products(partial, None, ((stacks.at[0], w0), (stacks.at[1], w1)))


def add_products(out, start, pairs):
    def step(at, _):
        cols = pl.ds(pl.multiple_of(at * 256, 256), 256)
        acc = added(*[dot(cells[...], w[:, cols]) for cells, w in pairs])
        if start is not None:
            acc = acc + start[:, cols]
        out[:, cols] = acc
        return 0

    lax.fori_loop(0, out.shape[1] // 256, step, 0)


def middle_kernel(stacks, partial, w2, out):
    add_products(out, partial, ((stacks.at[2], w2),))


def strand_kernel(stacks, partial, w3, ups, taps, grads, ahead, behind, sums, values, mixes, *, first):
    total = stacks.shape[1] // 2
    rows = total - 2 * EDGE
    units = sums.shape[1]
    count = units // LANES
    turn = turning(LANES)

    def project(at, _):
        near = pl.ds(pl.multiple_of(at * 256, 256), 256)
        cols = pl.ds(pl.multiple_of(first + at * 256, 256), 256)
        acc = partial[:, cols] + dot(stacks[3], w3[:, cols])
        acc = acc.astype(jnp.bfloat16).astype(jnp.float32)
        for way in range(2):
            base = way * total
            halo = 2 * rows + way * 2 * EDGE
            values[base : base + EDGE, near] = acc[halo : halo + EDGE]
            values[base + EDGE : base + EDGE + rows, near] = acc[way * rows : (way + 1) * rows]
            values[base + EDGE + rows : base + total, near] = acc[halo + EDGE : halo + 2 * EDGE]
        return 0

    lax.fori_loop(0, units // 256, project, 0)
    sums[...] = jnp.zeros(sums.shape, jnp.float32)

    def work(at, _):
        near = pl.ds(pl.multiple_of(at * LANES, LANES), LANES)
        cols = pl.ds(pl.multiple_of(first + at * LANES, LANES), LANES)
        for way in range(2):
            base = way * total
            places = [base + EDGE + (tap - REACH if way == 0 else REACH - tap) for tap in range(TAPS)]
            linear = values[base : base + total, near]
            logistic = jax.nn.sigmoid(linear)
            gating = linear * logistic
            up = ups[base : base + total, cols]
            grad_mix = up * gating
            mixes[way] = grad_mix
            mid = slice(EDGE, EDGE + rows)
            linear, logistic, gating, up, grad_mix = [
                cells[mid] for cells in (linear, logistic, gating, up, grad_mix)
            ]
            mixing = jnp.zeros((rows, LANES), jnp.float32)
            for tap in range(TAPS):
                moved = values[places[tap] : places[tap] + rows, near]
                mixing = mixing + taps[tap : tap + 1, cols] * moved
                sums[tap : tap + 1, near] += jnp.sum(grad_mix * moved, axis=0, keepdims=True)
            strand_out = mixing * gating
            acc = up * mixing * logistic * (1.0 + linear * (1.0 - logistic))
            for tap in range(TAPS):
                lower = 2 * EDGE - places[tap] + base
                acc = acc + taps[tap : tap + 1, cols] * mixes[way, lower : lower + rows]
            grads[way * rows : (way + 1) * rows, near] = acc.astype(jnp.bfloat16)
            if way == 0:
                ahead[:, near] = strand_out
            else:
                far = pl.ds(pl.multiple_of((count - 1 - at) * LANES, LANES), LANES)
                behind[:, far] = dot(strand_out.astype(jnp.bfloat16), turn)
        return 0

    lax.fori_loop(0, count, work, 0)


def product_kernel(columns, *refs, block, parts):
    grads, refs = refs[:parts], refs[parts:]
    out = refs[-1]
    start = 0
    for part in grads:
        stop = start + part.shape[1]
        out[:, start:stop] = dot(columns[block], part[...]).astype(out.dtype)
        start = stop
    if len(refs) > 1:
        out[:, start:] = refs[0][...]


def merge_kernel(columns, came, *refs, block, parts):
    grads, refs = refs[:parts], refs[parts:]
    out = refs[-1]
    start = 0
    for part in grads:
        stop = start + part.shape[1]
        own = dot(columns[block], part[...])
        out[:, start:stop] = (own + came[:, start:stop].astype(jnp.float32)).astype(jnp.bfloat16)
        start = stop
    if len(refs) > 1:
        out[:, start:] = paired(added(refs[0][...], came[:, start:])).astype(jnp.bfloat16)


def small_kernel(place, hot, w0, w1, w2, w3, *refs):
    parts, (out, grads, sums, table) = refs[:6], refs[6:]
    rows = hot.shape[1] // 3
    start = 0
    for at in range(3):
        part, part_sums = parts[at * 2], parts[at * 2 + 1]
        stop = start + part.shape[1]
        grads[:8, start:stop] = dot(hot[:, :rows], part[:rows])[:8]
        grads[8:, start:stop] = dot(hot[:, :rows], part[rows:])[:8]
        sums[:, start:stop] = part_sums[...]
        start = stop
    split = jnp.concatenate(thirds(grads[...]), axis=0)
    turn = turning(256)
    width = w0.shape[0]
    dims = (((1,), (1,)), ((), ()))
    backs = []
    for w in (w0, w1, w2, w3):
        back = lax.dot_general(split, w[...], dims, preferred_element_type=jnp.float32)
        backs.append(back[:16] + back[16:32] + back[32:])
    for r in range(4):
        cols = pl.ds(pl.multiple_of((place[0] ^ r) * width, width), width)
        there = turned(jnp.concatenate(thirds(backs[3 - r][8:]), axis=0), turn)
        table[:, cols] = backs[r][:8] + there[:8] + there[8:16] + there[16:]
    units = sums.shape[1]
    count = units // LANES
    for at in range(count):
        pack = jnp.concatenate(
            [
                sums[:, at * LANES : (at + 1) * LANES],
                table[:, at * LANES : (at + 1) * LANES],
                table[:, units + at * LANES : units + (at + 1) * LANES],
                jnp.zeros((8, LANES), jnp.float32),
            ],
            axis=0,
        )
        head = pack.astype(jnp.bfloat16).astype(jnp.float32)
        rest = pack - head
        low = low_lanes(pack.shape)
        first = jnp.where(low, head, pltpu.roll(rest, LANES // 2, 1))
        second = jnp.where(low, pltpu.roll(head, LANES // 2, 1), rest)
        out[at * PACK : (at + 1) * PACK] = first.astype(jnp.bfloat16)
        out[(count + at) * PACK : (count + at + 1) * PACK] = second.astype(jnp.bfloat16)


def back_kernel(place, w0, w1, w2, w3, later, *refs):
    parts, (out, block, backs, grads) = refs[:9], refs[9:]
    rows = out.shape[0]
    width = w0.shape[0]
    turn = turning(256)
    dims = (((1,), (1,)), ((), ()))
    start = 0
    for at in range(3):
        part = parts[at * 3]
        stop = start + part.shape[1]
        grads[:, start:stop] = part[...]
        start = stop
    forward = jnp.concatenate([parts[at * 3 + 1][...] for at in range(3)], axis=1)
    backward = jnp.concatenate([parts[at * 3 + 2][...] for at in (2, 1, 0)], axis=1)
    block[...] = (forward + backward).astype(jnp.bfloat16)
    for r, w in enumerate((w0, w1, w2, w3)):
        backs[r] = lax.dot_general(grads[...], w[...], dims, preferred_element_type=jnp.float32)
    for r in range(4):
        whole = backs[r, :rows] + turned(backs[3 - r, rows:].astype(jnp.bfloat16), turn)
        out[:, pl.ds(pl.multiple_of((place[0] ^ r) * width, width), width)] = whole.astype(jnp.bfloat16)


def block_kernel(place, columns, mate, came, *refs, parts):
    grads, refs = refs[:parts], refs[parts:]
    wide = len(refs) > 5
    if wide:
        merged, outs, own, extra = refs[0], refs[1:5], refs[5], refs[6]
        extra[...] = paired(added(merged[:, own.shape[1] :], came[:, own.shape[1] :]))
    else:
        outs, own = refs[:4], refs[4]
    rows = outs[0].shape[0]
    units = own.shape[1]
    product_kernel(columns, *grads, own, block=0, parts=parts)
    for step, out in enumerate(outs):
        here = pl.ds(pl.multiple_of((place[1] + step) % 4 * rows, rows), rows)
        out[:, :units] = added(own[here], mate[here], came[here, :units]).astype(jnp.bfloat16)
        if wide:
            out[:, units:] = extra[here].astype(jnp.bfloat16)


def quarter_kernel(*refs):
    head, tail, out = refs[:4], refs[4:8], refs[8]
    rows, units = head[0].shape
    size = 32

    def step(at, _):
        here = pl.ds(pl.multiple_of(at * size, size), size)
        out[here, :units] = added(*[part[here] for part in head]).astype(jnp.bfloat16)
        cells = added(*[part[here] for part in tail])
        out[here, units : 2 * units] = cells[:, :units].astype(jnp.bfloat16)
        out[here, 2 * units :] = paired(cells[:, units:]).astype(jnp.bfloat16)
        return 0

    lax.fori_loop(0, rows // size, step, 0)


def piece_kernel(parts, out):
    units = out.shape[2] - LANES
    total = parts[0].astype(jnp.float32)
    for at in range(1, parts.shape[0]):
        total = total + parts[at].astype(jnp.float32)
    plain = total[:, :units].astype(jnp.bfloat16)
    packed = paired(total[:, units:]).astype(jnp.bfloat16)
    for at in range(parts.shape[0]):
        out[at, :, :units] = plain
        out[at, :, units:] = packed


def write_quarters(place, quarters, weight_out, cells, done, factor):
    rows = cells.shape[1]
    units = cells.shape[2]
    copies = []
    for at, (step, part) in enumerate(quarters):
        cells[at] = part[:, :units].astype(jnp.float32) * factor
        there = pl.ds(pl.multiple_of((place[1] + 4 - step) % 4 * rows, rows), rows)
        copies.append(pltpu.make_async_copy(cells.at[at], weight_out.at[there], done.at[at]))
        copies[-1].start()
    return copies


def first_kernel(place, q0, q3, weight_out, cells, done, *, factor):
    for copy in write_quarters(place, ((0, q0), (3, q3)), weight_out, cells, done, factor):
        copy.wait()


def final_kernel(
    place, q0, q1, q2, q3, begun, weight_out, taps_out, table_out, packed, cells, done, *, factor
):
    copies = write_quarters(place, ((1, q1), (2, q2)), weight_out, cells, done, factor)
    rows = q0.shape[0]
    units = cells.shape[2]
    for step, part in enumerate((q0, q1, q2, q3)):
        there = pl.ds(pl.multiple_of((place[1] + 4 - step) % 4 * rows, rows), rows)
        packed[there] = part[:, units:].astype(jnp.float32)
    cells = packed[...]
    whole = cells + pltpu.roll(cells, LANES // 2, 1)
    half = whole.shape[0] // 2
    whole = jnp.where(low_lanes((half, LANES)), whole[:half], whole[half:]) * factor
    count = half // PACK
    symbols = table_out.shape[0]
    for at in range(count):
        cols = slice(at * LANES, (at + 1) * LANES)
        taps_out[:, cols] = whole[at * PACK : at * PACK + TAPS]
        table_out[:, cols] = whole[at * PACK + 8 : at * PACK + 8 + symbols]
        cols = slice(units + at * LANES, units + (at + 1) * LANES)
        table_out[:, cols] = whole[at * PACK + 16 : at * PACK + 16 + symbols]
    for copy in copies:
        copy.wait()


def call(kernel, outs, *args, scratch=(), scalar=False, unread=(), far=(), aliases=None, **fixed):
    inside = pl.BlockSpec(memory_space=pltpu.VMEM)
    specs = [inside] * len(args)
    if scalar:
        specs[0] = pl.BlockSpec(memory_space=pltpu.SMEM)
    for at in unread:
        specs[at] = pl.BlockSpec(memory_space=pl.ANY)
    return pl.pallas_call(
        functools.partial(kernel, **fixed),
        out_shape=outs,
        in_specs=specs,
        out_specs=far or jax.tree.map(lambda _: inside, outs),
        input_output_aliases=aliases or {},
        scratch_shapes=list(scratch),
        compiler_params=pltpu.CompilerParams(vmem_limit_bytes=20 * 2**20),
    )(*args)


def array(shape, dtype=jnp.bfloat16):
    return jax.ShapeDtypeStruct(shape, dtype)


def step(hidden, tokens, embedding, weight, kernel, cotangent):
    window = hidden[0]
    upstream = cotangent[0]
    rows, features = window.shape
    units = weight.shape[1]
    symbols = embedding.shape[0]
    factor = 1.0 / math.sqrt(rows * 256)
    width = features // 4
    total = rows + 2 * EDGE
    me = 2 * lax.axis_index("xl") + lax.axis_index("c")
    place = jnp.stack([me, lax.axis_index("y")]).astype(jnp.int32)
    weights = [weight, swap_core(weight), side(weight)]
    weights.append(swap_core(weights[2]))
    top = pl.BlockSpec((EDGE, features), lambda at: (0, 0))
    bottom = pl.BlockSpec((EDGE, features), lambda at: (rows // EDGE - 1, 0))
    up_top = pl.BlockSpec((EDGE, units), lambda at: (0, 0))
    up_bottom = pl.BlockSpec((EDGE, units), lambda at: (rows // EDGE - 1, 0))
    edge = array((EDGE, features + units))
    before, after = pl.pallas_call(
        edge_kernel,
        out_shape=(edge, edge),
        grid=(1,),
        in_specs=[
            pl.BlockSpec(memory_space=pltpu.SMEM),
            bottom,
            top,
            up_bottom,
            up_top,
            pl.BlockSpec((symbols, features), lambda at: (0, 0)),
        ],
        out_specs=[pl.BlockSpec(edge.shape, lambda at: (0, 0))] * 2,
        scratch_shapes=[pltpu.VMEM((EDGE, features), jnp.float32)],
    )(tokens, window, window, upstream, upstream, embedding)
    before = shift(before, ("xh", "z", "y"), neighbour(1))
    after = shift(after, ("xh", "z", "y"), neighbour(-1))
    centre, columns, up_centre, taps, hot = call(
        centre_kernel,
        (
            array((4, 2 * rows, width)),
            array((4, width, 2 * rows)),
            array((2 * rows, units), jnp.float32),
            array(kernel.shape, jnp.float32),
            array((16, 3 * rows)),
        ),
        place,
        tokens,
        kernel,
        window,
        embedding,
        upstream,
        scalar=True,
        unread=(3, 4, 5),
        scratch=(
            pltpu.VMEM((rows, features), jnp.bfloat16),
            pltpu.VMEM((symbols, features), jnp.float32),
            pltpu.VMEM((rows, units), jnp.bfloat16),
            pltpu.SemaphoreType.DMA((3,)),
        ),
    )
    wide = array((2 * total, units), jnp.float32)
    stacks, ups, partial = call(
        early_kernel,
        (array((4, 2 * total, width)), wide, wide),
        place,
        centre,
        up_centre,
        before,
        after,
        *weights[:2],
        scalar=True,
    )
    partial = call(middle_kernel, wide, stacks, partial, weights[2])
    ends = (0, units // 2, units // 4 * 3, units)
    parts = []
    for at in range(3):
        size = ends[at + 1] - ends[at]
        parts.append(
            call(
                strand_kernel,
                (
                    array((2 * rows, size)),
                    array((rows, size), jnp.float32),
                    array((rows, size), jnp.float32),
                    array((8, size), jnp.float32),
                ),
                stacks,
                partial,
                weights[3],
                ups,
                taps,
                scratch=(pltpu.VMEM((2 * total, size), jnp.float32), pltpu.VMEM((2, total, LANES), jnp.float32)),
                first=ends[at],
            )
        )
    grads = [[parts[0][0]], [parts[1][0], parts[2][0]]]
    extra = call(
        small_kernel,
        array((width, LANES)),
        place,
        hot,
        *weights,
        *[cells for part in parts for cells in (part[0], part[3])],
        scalar=True,
        scratch=(
            pltpu.VMEM((16, units), jnp.float32),
            pltpu.VMEM((8, units), jnp.float32),
            pltpu.VMEM((8, features), jnp.float32),
        ),
    )
    chunk = array((width, units // 2))
    came = []
    mates = []
    for at in range(2):
        count = len(grads[at])
        rest = [extra] * at
        large = array((width, units // 2 + LANES * at))
        goes = call(product_kernel, large, columns, *grads[at], *rest, block=3, parts=count)
        goes = swap_core(goes)
        merged = call(merge_kernel, large, columns, goes, *grads[at], *rest, block=2, parts=count)
        came.append(side(merged))
        mate = call(product_kernel, chunk, columns, *grads[at], block=1, parts=count)
        mates.append(swap_core(mate))
    part = width // 4
    own = pltpu.VMEM(chunk.shape, jnp.float32)
    head = call(
        block_kernel,
        (array((part, units // 2)),) * 4,
        place,
        columns,
        mates[0],
        came[0],
        *grads[0],
        scalar=True,
        scratch=(own,),
        parts=1,
    )
    head = [head[0]] + [along_y(head[step], step) for step in (1, 2, 3)]
    tail = call(
        block_kernel,
        (array((part, units // 2 + LANES)),) * 4,
        place,
        columns,
        mates[1],
        came[1],
        *grads[1],
        merged,
        scalar=True,
        scratch=(own, pltpu.VMEM((width, LANES), jnp.float32)),
        parts=2,
    )
    grad_hidden, block_result = call(
        back_kernel,
        (array((rows, features)), array((rows, units))),
        place,
        *weights,
        tail[0],
        *[cells for part in parts for cells in part[:3]],
        scalar=True,
        unread=(5,),
        scratch=(pltpu.VMEM((4, 2 * rows, width), jnp.float32), pltpu.VMEM((2 * rows, units), jnp.bfloat16)),
    )
    tail = [tail[0]] + [along_y(tail[step], step) for step in (1, 2, 3)]
    quarter = call(quarter_kernel, array((part, units + LANES)), *head, *tail)
    pieces = quarter.reshape(16, part // 16, -1)
    pieces = lax.all_to_all(pieces, ("xh", "z"), split_axis=0, concat_axis=0, tiled=True)
    pieces = call(piece_kernel, array(pieces.shape), pieces)
    pieces = lax.all_to_all(pieces, ("xh", "z"), split_axis=0, concat_axis=0, tiled=True)
    quarter = pieces.reshape(quarter.shape)
    quarters = [quarter] + [along_y(quarter, step) for step in (1, 2, 3)]
    inside = pl.BlockSpec(memory_space=pltpu.VMEM)
    outside = pl.BlockSpec(memory_space=pl.ANY)
    spare = (pltpu.VMEM((2, part, units), jnp.float32), pltpu.SemaphoreType.DMA((2,)))
    begun = call(
        first_kernel,
        array((width, units), jnp.float32),
        place,
        quarters[0],
        quarters[3],
        scalar=True,
        far=outside,
        scratch=spare,
        factor=factor,
    )
    grad_weight, grad_kernel, grad_embedding = call(
        final_kernel,
        (array((width, units), jnp.float32), array(kernel.shape, jnp.float32), array(embedding.shape, jnp.float32)),
        place,
        *quarters,
        begun,
        scalar=True,
        unread=(5,),
        far=[outside, inside, inside],
        aliases={5: 0},
        scratch=(pltpu.VMEM((width, LANES), jnp.float32), *spare),
        factor=factor,
    )
    return block_result[None], grad_hidden[None], grad_weight, grad_kernel, grad_embedding


def solution(mesh):
    fine = Mesh(mesh.devices.reshape(SIZES), AXES)
    batch = ("xl", "c")
    spot = ("xh", "z", "y")
    in_specs = (P(batch, spot, None), P(batch, spot), P(), P(batch, None), P(), P(batch, spot, None))
    out_specs = (P(batch, spot, None), P(batch, spot, None), P(batch, None), P(), P())
    return jax.shard_map(step, mesh=fine, in_specs=in_specs, out_specs=out_specs, check_vma=False)
```

```python
import functools
import math

import jax
import jax.numpy as jnp
import numpy as np
from jax import lax
from jax.experimental import pallas as pl
from jax.experimental.pallas import tpu as pltpu
from jax.sharding import Mesh, PartitionSpec as P


AXES = ("xl", "c", "xh", "z", "y")
SIZES = (2, 2, 2, 8, 4)
EDGE = 8
REACH = 3
TAPS = 7
LANES = 128
PACK = 32


def shift(cells, axes, target):
    sizes = [SIZES[AXES.index(axis)] for axis in axes]
    pairs = []
    for place in np.ndindex(*sizes):
        goal = target(*place)
        if goal is not None:
            pairs.append((int(np.ravel_multi_index(place, sizes)), int(np.ravel_multi_index(goal, sizes))))
    return lax.ppermute(cells, axes if len(axes) > 1 else axes[0], pairs)


def swap_core(cells):
    return shift(cells, ("c",), lambda c: (1 - c,))


def side(cells):
    def target(xl, c, xh):
        x = (2 * xh + xl + (1 if c == 0 else 3)) % 4
        return (x % 2, c, x // 2)

    return shift(cells, ("xl", "c", "xh"), target)


def along_y(cells, step):
    return shift(cells, ("y",), lambda y: ((y + step) % 4,))


def neighbour(step):
    def target(xh, z, y):
        place = (xh * 8 + z) * 4 + y + step
        if not 0 <= place < 64:
            return None
        return (place // 32, place // 4 % 8, place % 4)

    return target


def added(*parts):
    total = parts[0].astype(jnp.float32)
    for part in parts[1:]:
        total = total + part.astype(jnp.float32)
    return total


def low_lanes(shape):
    return lax.broadcasted_iota(jnp.int32, shape, len(shape) - 1) < LANES // 2


def paired(cells):
    whole = cells + pltpu.roll(cells, LANES // 2, 1)
    head = whole.astype(jnp.bfloat16).astype(jnp.float32)
    return jnp.where(low_lanes(cells.shape), head, whole - head)


def thirds(cells):
    head = cells.astype(jnp.bfloat16)
    rest = cells - head.astype(jnp.float32)
    middle = rest.astype(jnp.bfloat16)
    return head, middle, (rest - middle.astype(jnp.float32)).astype(jnp.bfloat16)


def turning(size):
    place = lax.broadcasted_iota(jnp.int32, (size, size), 0) + lax.broadcasted_iota(jnp.int32, (size, size), 1)
    return (place == size - 1).astype(jnp.bfloat16)


def dot(a, b):
    return jnp.dot(a, b, preferred_element_type=jnp.float32)


def turned(cells, turn):
    size = turn.shape[0]
    count = cells.shape[1] // size
    return jnp.concatenate([dot(cells[:, at * size : (at + 1) * size], turn) for at in range(count)[::-1]], axis=1)


def edge_kernel(codes, last, first, up_last, up_first, table, before, after, looked):
    rows = codes.shape[1]
    features = table.shape[1]
    for start, cells, up, out in ((rows - EDGE, last, up_last, before), (0, first, up_first, after)):
        for at in range(EDGE):
            looked[at : at + 1] = table[pl.ds(codes[0, start + at], 1)]
        out[:, :features] = (cells[...].astype(jnp.float32) + looked[...]).astype(jnp.bfloat16)
        out[:, features:] = up[...]


def centre_kernel(
    place, codes, taps, window_far, table_far, up_far, stacks, columns, ups, taps_near, hot, window, table, up, done
):
    loads = [
        pltpu.make_async_copy(far, near, done.at[at])
        for at, (far, near) in enumerate(((window_far, window), (table_far, table), (up_far, up)))
    ]
    for load in loads:
        load.start()
    taps_near[...] = taps[...]
    rows, features = window.shape
    symbol = lax.broadcasted_iota(jnp.int32, (16, rows), 0)
    one_hot = jnp.where(symbol == codes[...], 1.0, 0.0).astype(jnp.bfloat16)
    for at in range(3):
        hot[:, at * rows : (at + 1) * rows] = one_hot
    width = features // 4
    turn = turning(256)
    by_row = jnp.broadcast_to(codes[...].astype(jnp.float32), (rows, rows)).T
    by_row = jnp.concatenate([by_row] * (width // rows), axis=1)
    for load in loads:
        load.wait()
    for r in range(4):
        cols = pl.ds(pl.multiple_of((place[0] ^ r) * width, width), width)
        looked = jnp.zeros((rows, width), jnp.float32)
        for symbol in range(table.shape[0]):
            looked = looked + jnp.where(by_row == symbol, table[symbol : symbol + 1, cols], 0.0)
        middle = (window[:, cols].astype(jnp.float32) + looked).astype(jnp.bfloat16)
        back = turned(middle, turn)
        stacks[r, :rows] = middle
        stacks[3 - r, rows:] = back.astype(jnp.bfloat16)
        columns[r, :, :rows] = middle.astype(jnp.float32).T.astype(jnp.bfloat16)
        columns[3 - r, :, rows:] = back.T.astype(jnp.bfloat16)
    ups[:rows] = up[...].astype(jnp.float32)
    ups[rows:] = turned(up[...], turn)


def early_kernel(centre, w0, w1, partial):
    add_products(partial, None, ((centre.at[0], w0), (centre.at[1], w1)))


def halo_kernel(place, before, after, w0, w1, halos, ups, partial):
    width = halos.shape[2]
    features = 4 * width
    size = 2 * EDGE
    turn = turning(256)
    for r in range(4):
        cols = pl.ds(pl.multiple_of((place[0] ^ r) * width, width), width)
        rows = jnp.concatenate([before[:, cols].astype(jnp.float32), after[:, cols].astype(jnp.float32)], axis=0)
        rows = rows.astype(jnp.bfloat16)
        halos[r, :size] = rows
        halos[3 - r, size:] = turned(rows, turn).astype(jnp.bfloat16)
    up = jnp.concatenate(
        [before[:, features:].astype(jnp.float32), after[:, features:].astype(jnp.float32)], axis=0
    ).astype(jnp.bfloat16)
    ups[:size] = up.astype(jnp.float32)
    ups[size:] = turned(up, turn)
    add_products(partial, None, ((halos.at[0], w0), (halos.at[1], w1)))


def add_products(out, start, pairs):
    def step(at, _):
        cols = pl.ds(pl.multiple_of(at * 256, 256), 256)
        acc = added(*[dot(cells[...], w[:, cols]) for cells, w in pairs])
        if start is not None:
            acc = acc + start[:, cols]
        out[:, cols] = acc
        return 0

    lax.fori_loop(0, out.shape[1] // 256, step, 0)


def middle_kernel(centre, halos, partial, partial_halo, w2, out, rows):
    size = centre.shape[1]
    rows[:size] = centre[2]
    rows[size:] = halos[2]

    def step(at, _):
        cols = pl.ds(pl.multiple_of(at * 256, 256), 256)
        start = jnp.concatenate([partial[:, cols], partial_halo[:, cols]], axis=0)
        out[:, cols] = start + dot(rows[...], w2[:, cols])
        return 0

    lax.fori_loop(0, out.shape[1] // 256, step, 0)


def strand_kernel(
    centre, halos, partial, w3, ups, ups_halo, taps, grads, ahead, behind, sums, values, mixes, stack, *, first
):
    rows = centre.shape[1] // 2
    total = rows + 2 * EDGE
    units = sums.shape[1]
    stack[: 2 * rows] = centre[3]
    stack[2 * rows :] = halos[3]
    count = units // LANES
    turn = turning(LANES)

    def project(at, _):
        near = pl.ds(pl.multiple_of(at * 256, 256), 256)
        cols = pl.ds(pl.multiple_of(first + at * 256, 256), 256)
        acc = partial[:, cols] + dot(stack[...], w3[:, cols])
        acc = acc.astype(jnp.bfloat16).astype(jnp.float32)
        for way in range(2):
            base = way * total
            halo = 2 * rows + way * 2 * EDGE
            values[base : base + EDGE, near] = acc[halo : halo + EDGE]
            values[base + EDGE : base + EDGE + rows, near] = acc[way * rows : (way + 1) * rows]
            values[base + EDGE + rows : base + total, near] = acc[halo + EDGE : halo + 2 * EDGE]
        return 0

    lax.fori_loop(0, units // 256, project, 0)
    sums[...] = jnp.zeros(sums.shape, jnp.float32)

    def work(at, _):
        near = pl.ds(pl.multiple_of(at * LANES, LANES), LANES)
        cols = pl.ds(pl.multiple_of(first + at * LANES, LANES), LANES)
        for way in range(2):
            base = way * total
            places = [base + EDGE + (tap - REACH if way == 0 else REACH - tap) for tap in range(TAPS)]
            linear = values[base : base + total, near]
            logistic = jax.nn.sigmoid(linear)
            gating = linear * logistic
            halo = way * 2 * EDGE
            up = jnp.concatenate(
                [
                    ups_halo[halo : halo + EDGE, cols],
                    ups[way * rows : (way + 1) * rows, cols],
                    ups_halo[halo + EDGE : halo + 2 * EDGE, cols],
                ],
                axis=0,
            )
            grad_mix = up * gating
            mixes[way] = grad_mix
            mid = slice(EDGE, EDGE + rows)
            linear, logistic, gating, up, grad_mix = [
                cells[mid] for cells in (linear, logistic, gating, up, grad_mix)
            ]
            mixing = jnp.zeros((rows, LANES), jnp.float32)
            for tap in range(TAPS):
                moved = values[places[tap] : places[tap] + rows, near]
                mixing = mixing + taps[tap : tap + 1, cols] * moved
                sums[tap : tap + 1, near] += jnp.sum(grad_mix * moved, axis=0, keepdims=True)
            strand_out = mixing * gating
            acc = up * mixing * logistic * (1.0 + linear * (1.0 - logistic))
            for tap in range(TAPS):
                lower = 2 * EDGE - places[tap] + base
                acc = acc + taps[tap : tap + 1, cols] * mixes[way, lower : lower + rows]
            grads[way * rows : (way + 1) * rows, near] = acc.astype(jnp.bfloat16)
            if way == 0:
                ahead[:, near] = strand_out
            else:
                far = pl.ds(pl.multiple_of((count - 1 - at) * LANES, LANES), LANES)
                behind[:, far] = dot(strand_out.astype(jnp.bfloat16), turn)
        return 0

    lax.fori_loop(0, count, work, 0)


def product_kernel(columns, *refs, block, parts):
    grads, refs = refs[:parts], refs[parts:]
    out = refs[-1]
    start = 0
    for part in grads:
        stop = start + part.shape[1]
        out[:, start:stop] = dot(columns[block], part[...]).astype(out.dtype)
        start = stop
    if len(refs) > 1:
        out[:, start:] = refs[0][...]


def merge_kernel(columns, came, *refs, block, parts):
    grads, refs = refs[:parts], refs[parts:]
    out = refs[-1]
    start = 0
    for part in grads:
        stop = start + part.shape[1]
        own = dot(columns[block], part[...])
        out[:, start:stop] = (own + came[:, start:stop].astype(jnp.float32)).astype(jnp.bfloat16)
        start = stop
    if len(refs) > 1:
        out[:, start:] = paired(added(refs[0][...], came[:, start:])).astype(jnp.bfloat16)


def small_kernel(place, hot, w0, w1, w2, w3, *refs):
    parts, (out, grads, sums, table) = refs[:6], refs[6:]
    rows = hot.shape[1] // 3
    start = 0
    for at in range(3):
        part, part_sums = parts[at * 2], parts[at * 2 + 1]
        stop = start + part.shape[1]
        grads[:8, start:stop] = dot(hot[:, :rows], part[:rows])[:8]
        grads[8:, start:stop] = dot(hot[:, :rows], part[rows:])[:8]
        sums[:, start:stop] = part_sums[...]
        start = stop
    split = jnp.concatenate(thirds(grads[...]), axis=0)
    turn = turning(256)
    width = w0.shape[0]
    dims = (((1,), (1,)), ((), ()))
    backs = []
    for w in (w0, w1, w2, w3):
        back = lax.dot_general(split, w[...], dims, preferred_element_type=jnp.float32)
        backs.append(back[:16] + back[16:32] + back[32:])
    for r in range(4):
        cols = pl.ds(pl.multiple_of((place[0] ^ r) * width, width), width)
        there = turned(jnp.concatenate(thirds(backs[3 - r][8:]), axis=0), turn)
        table[:, cols] = backs[r][:8] + there[:8] + there[8:16] + there[16:]
    units = sums.shape[1]
    count = units // LANES
    for at in range(count):
        pack = jnp.concatenate(
            [
                sums[:, at * LANES : (at + 1) * LANES],
                table[:, at * LANES : (at + 1) * LANES],
                table[:, units + at * LANES : units + (at + 1) * LANES],
                jnp.zeros((8, LANES), jnp.float32),
            ],
            axis=0,
        )
        head = pack.astype(jnp.bfloat16).astype(jnp.float32)
        rest = pack - head
        low = low_lanes(pack.shape)
        first = jnp.where(low, head, pltpu.roll(rest, LANES // 2, 1))
        second = jnp.where(low, pltpu.roll(head, LANES // 2, 1), rest)
        out[at * PACK : (at + 1) * PACK] = first.astype(jnp.bfloat16)
        out[(count + at) * PACK : (count + at + 1) * PACK] = second.astype(jnp.bfloat16)


def back_kernel(place, w0, w1, w2, w3, later, *refs):
    parts, (out, block, backs, grads) = refs[:9], refs[9:]
    rows = out.shape[0]
    width = w0.shape[0]
    turn = turning(256)
    dims = (((1,), (1,)), ((), ()))
    start = 0
    for at in range(3):
        part = parts[at * 3]
        stop = start + part.shape[1]
        grads[:, start:stop] = part[...]
        start = stop
    forward = jnp.concatenate([parts[at * 3 + 1][...] for at in range(3)], axis=1)
    backward = jnp.concatenate([parts[at * 3 + 2][...] for at in (2, 1, 0)], axis=1)
    block[...] = (forward + backward).astype(jnp.bfloat16)
    for r, w in enumerate((w0, w1, w2, w3)):
        backs[r] = lax.dot_general(grads[...], w[...], dims, preferred_element_type=jnp.float32)
    for r in range(4):
        whole = backs[r, :rows] + turned(backs[3 - r, rows:].astype(jnp.bfloat16), turn)
        out[:, pl.ds(pl.multiple_of((place[0] ^ r) * width, width), width)] = whole.astype(jnp.bfloat16)


def block_kernel(place, columns, mate, came, *refs, parts):
    grads, refs = refs[:parts], refs[parts:]
    wide = len(refs) > 5
    if wide:
        merged, outs, own, extra = refs[0], refs[1:5], refs[5], refs[6]
        extra[...] = paired(added(merged[:, own.shape[1] :], came[:, own.shape[1] :]))
    else:
        outs, own = refs[:4], refs[4]
    rows = outs[0].shape[0]
    units = own.shape[1]
    product_kernel(columns, *grads, own, block=0, parts=parts)
    for step, out in enumerate(outs):
        here = pl.ds(pl.multiple_of((place[1] + step) % 4 * rows, rows), rows)
        out[:, :units] = added(own[here], mate[here], came[here, :units]).astype(jnp.bfloat16)
        if wide:
            out[:, units:] = extra[here].astype(jnp.bfloat16)


def quarter_kernel(*refs):
    head, tail, out = refs[:4], refs[4:8], refs[8]
    rows, units = head[0].shape
    size = 32

    def step(at, _):
        here = pl.ds(pl.multiple_of(at * size, size), size)
        out[here, :units] = added(*[part[here] for part in head]).astype(jnp.bfloat16)
        cells = added(*[part[here] for part in tail])
        out[here, units : 2 * units] = cells[:, :units].astype(jnp.bfloat16)
        out[here, 2 * units :] = paired(cells[:, units:]).astype(jnp.bfloat16)
        return 0

    lax.fori_loop(0, rows // size, step, 0)


def piece_kernel(parts, out):
    units = out.shape[2] - LANES
    total = parts[0].astype(jnp.float32)
    for at in range(1, parts.shape[0]):
        total = total + parts[at].astype(jnp.float32)
    plain = total[:, :units].astype(jnp.bfloat16)
    packed = paired(total[:, units:]).astype(jnp.bfloat16)
    for at in range(parts.shape[0]):
        out[at, :, :units] = plain
        out[at, :, units:] = packed


def final_kernel(place, q0, q1, q2, q3, weight_out, taps_out, table_out, packed, *, factor):
    rows = q0.shape[0]
    units = weight_out.shape[1]
    for step, part in enumerate((q0, q1, q2, q3)):
        there = pl.ds(pl.multiple_of((place[1] + 4 - step) % 4 * rows, rows), rows)
        weight_out[there] = part[:, :units].astype(jnp.float32) * factor
        packed[there] = part[:, units:].astype(jnp.float32)
    cells = packed[...]
    whole = cells + pltpu.roll(cells, LANES // 2, 1)
    half = whole.shape[0] // 2
    whole = jnp.where(low_lanes((half, LANES)), whole[:half], whole[half:]) * factor
    count = half // PACK
    symbols = table_out.shape[0]
    for at in range(count):
        cols = slice(at * LANES, (at + 1) * LANES)
        taps_out[:, cols] = whole[at * PACK : at * PACK + TAPS]
        table_out[:, cols] = whole[at * PACK + 8 : at * PACK + 8 + symbols]
        cols = slice(units + at * LANES, units + (at + 1) * LANES)
        table_out[:, cols] = whole[at * PACK + 16 : at * PACK + 16 + symbols]


def call(kernel, outs, *args, scratch=(), scalar=False, unread=(), **fixed):
    inside = pl.BlockSpec(memory_space=pltpu.VMEM)
    specs = [inside] * len(args)
    if scalar:
        specs[0] = pl.BlockSpec(memory_space=pltpu.SMEM)
    for at in unread:
        specs[at] = pl.BlockSpec(memory_space=pltpu.HBM if kernel is centre_kernel else pl.ANY)
    return pl.pallas_call(
        functools.partial(kernel, **fixed),
        out_shape=outs,
        in_specs=specs,
        out_specs=jax.tree.map(lambda _: inside, outs),
        scratch_shapes=list(scratch),
        compiler_params=pltpu.CompilerParams(vmem_limit_bytes=20 * 2**20),
    )(*args)


def array(shape, dtype=jnp.bfloat16):
    return jax.ShapeDtypeStruct(shape, dtype)


def step(hidden, tokens, embedding, weight, kernel, cotangent):
    window = hidden[0]
    upstream = cotangent[0]
    rows, features = window.shape
    units = weight.shape[1]
    symbols = embedding.shape[0]
    factor = 1.0 / math.sqrt(rows * 256)
    width = features // 4
    total = rows + 2 * EDGE
    me = 2 * lax.axis_index("xl") + lax.axis_index("c")
    place = jnp.stack([me, lax.axis_index("y")]).astype(jnp.int32)
    weights = [weight, swap_core(weight), side(weight)]
    weights.append(swap_core(weights[2]))
    top = pl.BlockSpec((EDGE, features), lambda at: (0, 0))
    bottom = pl.BlockSpec((EDGE, features), lambda at: (rows // EDGE - 1, 0))
    up_top = pl.BlockSpec((EDGE, units), lambda at: (0, 0))
    up_bottom = pl.BlockSpec((EDGE, units), lambda at: (rows // EDGE - 1, 0))
    edge = array((EDGE, features + units))
    before, after = pl.pallas_call(
        edge_kernel,
        out_shape=(edge, edge),
        grid=(1,),
        in_specs=[
            pl.BlockSpec(memory_space=pltpu.SMEM),
            bottom,
            top,
            up_bottom,
            up_top,
            pl.BlockSpec((symbols, features), lambda at: (0, 0)),
        ],
        out_specs=[pl.BlockSpec(edge.shape, lambda at: (0, 0))] * 2,
        scratch_shapes=[pltpu.VMEM((EDGE, features), jnp.float32)],
    )(tokens, window, window, upstream, upstream, embedding)
    before = shift(before, ("xh", "z", "y"), neighbour(1))
    after = shift(after, ("xh", "z", "y"), neighbour(-1))
    centre, columns, up_centre, taps, hot = call(
        centre_kernel,
        (
            array((4, 2 * rows, width)),
            array((4, width, 2 * rows)),
            array((2 * rows, units), jnp.float32),
            array(kernel.shape, jnp.float32),
            array((16, 3 * rows)),
        ),
        place,
        tokens,
        kernel,
        window,
        embedding,
        upstream,
        scalar=True,
        unread=(3, 4, 5),
        scratch=(
            pltpu.VMEM((rows, features), jnp.bfloat16),
            pltpu.VMEM((symbols, features), jnp.float32),
            pltpu.VMEM((rows, units), jnp.bfloat16),
            pltpu.SemaphoreType.DMA((3,)),
        ),
    )
    partial = call(early_kernel, array((2 * rows, units), jnp.float32), centre, *weights[:2])
    halos, ups_halo, partial_halo = call(
        halo_kernel,
        (
            array((4, 4 * EDGE, width)),
            array((4 * EDGE, units), jnp.float32),
            array((4 * EDGE, units), jnp.float32),
        ),
        place,
        before,
        after,
        *weights[:2],
        scalar=True,
    )
    partial = call(
        middle_kernel,
        array((2 * total, units), jnp.float32),
        centre,
        halos,
        partial,
        partial_halo,
        weights[2],
        scratch=(pltpu.VMEM((2 * total, width), jnp.bfloat16),),
    )
    ends = (0, units // 2, units // 4 * 3, units)
    parts = []
    for at in range(3):
        size = ends[at + 1] - ends[at]
        parts.append(
            call(
                strand_kernel,
                (
                    array((2 * rows, size)),
                    array((rows, size), jnp.float32),
                    array((rows, size), jnp.float32),
                    array((8, size), jnp.float32),
                ),
                centre,
                halos,
                partial,
                weights[3],
                up_centre,
                ups_halo,
                taps,
                scratch=(
                    pltpu.VMEM((2 * total, size), jnp.float32),
                    pltpu.VMEM((2, total, LANES), jnp.float32),
                    pltpu.VMEM((2 * total, width), jnp.bfloat16),
                ),
                first=ends[at],
            )
        )
    grads = [[parts[0][0]], [parts[1][0], parts[2][0]]]
    extra = call(
        small_kernel,
        array((width, LANES)),
        place,
        hot,
        *weights,
        *[cells for part in parts for cells in (part[0], part[3])],
        scalar=True,
        scratch=(
            pltpu.VMEM((16, units), jnp.float32),
            pltpu.VMEM((8, units), jnp.float32),
            pltpu.VMEM((8, features), jnp.float32),
        ),
    )
    chunk = array((width, units // 2))
    came = []
    mates = []
    for at in range(2):
        count = len(grads[at])
        rest = [extra] * at
        large = array((width, units // 2 + LANES * at))
        goes = call(product_kernel, large, columns, *grads[at], *rest, block=3, parts=count)
        goes = swap_core(goes)
        merged = call(merge_kernel, large, columns, goes, *grads[at], *rest, block=2, parts=count)
        came.append(side(merged))
        mate = call(product_kernel, chunk, columns, *grads[at], block=1, parts=count)
        mates.append(swap_core(mate))
    part = width // 4
    own = pltpu.VMEM(chunk.shape, jnp.float32)
    head = call(
        block_kernel,
        (array((part, units // 2)),) * 4,
        place,
        columns,
        mates[0],
        came[0],
        *grads[0],
        scalar=True,
        scratch=(own,),
        parts=1,
    )
    head = [head[0]] + [along_y(head[step], step) for step in (1, 2, 3)]
    tail = call(
        block_kernel,
        (array((part, units // 2 + LANES)),) * 4,
        place,
        columns,
        mates[1],
        came[1],
        *grads[1],
        merged,
        scalar=True,
        scratch=(own, pltpu.VMEM((width, LANES), jnp.float32)),
        parts=2,
    )
    grad_hidden, block_result = call(
        back_kernel,
        (array((rows, features)), array((rows, units))),
        place,
        *weights,
        tail[0],
        *[cells for part in parts for cells in part[:3]],
        scalar=True,
        unread=(5,),
        scratch=(pltpu.VMEM((4, 2 * rows, width), jnp.float32), pltpu.VMEM((2 * rows, units), jnp.bfloat16)),
    )
    tail = [tail[0]] + [along_y(tail[step], step) for step in (1, 2, 3)]
    quarter = call(quarter_kernel, array((part, units + LANES)), *head, *tail)
    pieces = quarter.reshape(16, part // 16, -1)
    pieces = lax.all_to_all(pieces, ("xh", "z"), split_axis=0, concat_axis=0, tiled=True)
    pieces = call(piece_kernel, array(pieces.shape), pieces)
    pieces = lax.all_to_all(pieces, ("xh", "z"), split_axis=0, concat_axis=0, tiled=True)
    quarter = pieces.reshape(quarter.shape)
    quarters = [quarter] + [along_y(quarter, step) for step in (1, 2, 3)]
    grad_weight, grad_kernel, grad_embedding = call(
        final_kernel,
        (array((width, units), jnp.float32), array(kernel.shape, jnp.float32), array(embedding.shape, jnp.float32)),
        place,
        *quarters,
        scalar=True,
        scratch=(pltpu.VMEM((width, LANES), jnp.float32),),
        factor=factor,
    )
    return block_result[None], grad_hidden[None], grad_weight, grad_kernel, grad_embedding


def solution(mesh):
    fine = Mesh(mesh.devices.reshape(SIZES), AXES)
    batch = ("xl", "c")
    spot = ("xh", "z", "y")
    in_specs = (P(batch, spot, None), P(batch, spot), P(), P(batch, None), P(), P(batch, spot, None))
    out_specs = (P(batch, spot, None), P(batch, spot, None), P(batch, None), P(), P())
    return jax.shard_map(step, mesh=fine, in_specs=in_specs, out_specs=out_specs, check_vma=False)
```

```python
import functools
import math

import jax
import jax.numpy as jnp
import numpy as np
from jax import lax
from jax.experimental import pallas as pl
from jax.experimental.pallas import tpu as pltpu
from jax.sharding import Mesh, PartitionSpec as P


AXES = ("xl", "c", "xh", "z", "y")
SIZES = (2, 2, 2, 8, 4)
EDGE = 8
REACH = 3
TAPS = 7
LANES = 128
PACK = 32


def shift(cells, axes, target):
    sizes = [SIZES[AXES.index(axis)] for axis in axes]
    pairs = []
    for place in np.ndindex(*sizes):
        goal = target(*place)
        if goal is not None:
            pairs.append((int(np.ravel_multi_index(place, sizes)), int(np.ravel_multi_index(goal, sizes))))
    return lax.ppermute(cells, axes if len(axes) > 1 else axes[0], pairs)


def swap_core(cells):
    return shift(cells, ("c",), lambda c: (1 - c,))


def side(cells):
    def target(xl, c, xh):
        x = (2 * xh + xl + (1 if c == 0 else 3)) % 4
        return (x % 2, c, x // 2)

    return shift(cells, ("xl", "c", "xh"), target)


def along_y(cells, step):
    return shift(cells, ("y",), lambda y: ((y + step) % 4,))


def neighbour(step):
    def target(xh, z, y):
        place = (xh * 8 + z) * 4 + y + step
        if not 0 <= place < 64:
            return None
        return (place // 32, place // 4 % 8, place % 4)

    return target


def added(*parts):
    total = parts[0].astype(jnp.float32)
    for part in parts[1:]:
        total = total + part.astype(jnp.float32)
    return total


def low_lanes(shape):
    return lax.broadcasted_iota(jnp.int32, shape, len(shape) - 1) < LANES // 2


def paired(cells):
    whole = cells + pltpu.roll(cells, LANES // 2, 1)
    head = whole.astype(jnp.bfloat16).astype(jnp.float32)
    return jnp.where(low_lanes(cells.shape), head, whole - head)


def thirds(cells):
    head = cells.astype(jnp.bfloat16)
    rest = cells - head.astype(jnp.float32)
    middle = rest.astype(jnp.bfloat16)
    return head, middle, (rest - middle.astype(jnp.float32)).astype(jnp.bfloat16)


def turning(size):
    place = lax.broadcasted_iota(jnp.int32, (size, size), 0) + lax.broadcasted_iota(jnp.int32, (size, size), 1)
    return (place == size - 1).astype(jnp.bfloat16)


def dot(a, b):
    return jnp.dot(a, b, preferred_element_type=jnp.float32)


def turned(cells, turn):
    size = turn.shape[0]
    count = cells.shape[1] // size
    return jnp.concatenate([dot(cells[:, at * size : (at + 1) * size], turn) for at in range(count)[::-1]], axis=1)


def edge_kernel(codes, last, first, up_last, up_first, table, before, after, looked):
    rows = codes.shape[1]
    features = table.shape[1]
    for start, cells, up, out in ((rows - EDGE, last, up_last, before), (0, first, up_first, after)):
        for at in range(EDGE):
            looked[at : at + 1] = table[pl.ds(codes[0, start + at], 1)]
        out[:, :features] = (cells[...].astype(jnp.float32) + looked[...]).astype(jnp.bfloat16)
        out[:, features:] = up[...]


def centre_kernel(
    place,
    codes_far,
    taps_far,
    window_far,
    table_far,
    up_far,
    stacks,
    columns,
    ups,
    taps,
    hot,
    window,
    table,
    up,
    codes,
    done,
):
    loads = [
        pltpu.make_async_copy(far, near, done.at[at])
        for at, (far, near) in enumerate(
            ((window_far, window), (table_far, table), (up_far, up), (codes_far, codes), (taps_far, taps))
        )
    ]
    for load in loads:
        load.start()
    rows, features = window.shape
    turn = turning(256)
    width = features // 4
    for load in loads:
        load.wait()
    symbol = lax.broadcasted_iota(jnp.int32, (16, rows), 0)
    one_hot = jnp.where(symbol == codes[...], 1.0, 0.0).astype(jnp.bfloat16)
    for at in range(3):
        hot[:, at * rows : (at + 1) * rows] = one_hot
    by_row = jnp.broadcast_to(codes[...].astype(jnp.float32), (rows, rows)).T
    by_row = jnp.concatenate([by_row] * (width // rows), axis=1)
    for r in range(4):
        cols = pl.ds(pl.multiple_of((place[0] ^ r) * width, width), width)
        looked = jnp.zeros((rows, width), jnp.float32)
        for symbol in range(table.shape[0]):
            looked = looked + jnp.where(by_row == symbol, table[symbol : symbol + 1, cols], 0.0)
        middle = (window[:, cols].astype(jnp.float32) + looked).astype(jnp.bfloat16)
        back = turned(middle, turn)
        stacks[r, :rows] = middle
        stacks[3 - r, rows:] = back.astype(jnp.bfloat16)
        columns[r, :, :rows] = middle.astype(jnp.float32).T.astype(jnp.bfloat16)
        columns[3 - r, :, rows:] = back.T.astype(jnp.bfloat16)
    ups[:rows] = up[...].astype(jnp.float32)
    ups[rows:] = turned(up[...], turn)


def early_kernel(centre, w0, w1, partial):
    add_products(partial, None, ((centre.at[0], w0), (centre.at[1], w1)))


def halo_kernel(place, before, after, w0, w1, halos, ups, partial):
    width = halos.shape[2]
    features = 4 * width
    size = 2 * EDGE
    turn = turning(256)
    for r in range(4):
        cols = pl.ds(pl.multiple_of((place[0] ^ r) * width, width), width)
        rows = jnp.concatenate([before[:, cols].astype(jnp.float32), after[:, cols].astype(jnp.float32)], axis=0)
        rows = rows.astype(jnp.bfloat16)
        halos[r, :size] = rows
        halos[3 - r, size:] = turned(rows, turn).astype(jnp.bfloat16)
    up = jnp.concatenate(
        [before[:, features:].astype(jnp.float32), after[:, features:].astype(jnp.float32)], axis=0
    ).astype(jnp.bfloat16)
    ups[:size] = up.astype(jnp.float32)
    ups[size:] = turned(up, turn)
    add_products(partial, None, ((halos.at[0], w0), (halos.at[1], w1)))


def add_products(out, start, pairs):
    def step(at, _):
        cols = pl.ds(pl.multiple_of(at * 256, 256), 256)
        acc = added(*[dot(cells[...], w[:, cols]) for cells, w in pairs])
        if start is not None:
            acc = acc + start[:, cols]
        out[:, cols] = acc
        return 0

    lax.fori_loop(0, out.shape[1] // 256, step, 0)


def middle_kernel(centre, halos, partial, partial_halo, w2, out, rows):
    size = centre.shape[1]
    rows[:size] = centre[2]
    rows[size:] = halos[2]

    def step(at, _):
        cols = pl.ds(pl.multiple_of(at * 256, 256), 256)
        start = jnp.concatenate([partial[:, cols], partial_halo[:, cols]], axis=0)
        out[:, cols] = start + dot(rows[...], w2[:, cols])
        return 0

    lax.fori_loop(0, out.shape[1] // 256, step, 0)


def strand_kernel(
    centre, halos, partial, w3, ups, ups_halo, taps, grads, ahead, behind, sums, values, mixes, stack, *, first
):
    rows = centre.shape[1] // 2
    total = rows + 2 * EDGE
    units = sums.shape[1]
    stack[: 2 * rows] = centre[3]
    stack[2 * rows :] = halos[3]
    count = units // LANES
    turn = turning(LANES)

    def project(at, _):
        near = pl.ds(pl.multiple_of(at * 256, 256), 256)
        cols = pl.ds(pl.multiple_of(first + at * 256, 256), 256)
        acc = partial[:, cols] + dot(stack[...], w3[:, cols])
        acc = acc.astype(jnp.bfloat16).astype(jnp.float32)
        for way in range(2):
            base = way * total
            halo = 2 * rows + way * 2 * EDGE
            values[base : base + EDGE, near] = acc[halo : halo + EDGE]
            values[base + EDGE : base + EDGE + rows, near] = acc[way * rows : (way + 1) * rows]
            values[base + EDGE + rows : base + total, near] = acc[halo + EDGE : halo + 2 * EDGE]
        return 0

    lax.fori_loop(0, units // 256, project, 0)
    sums[...] = jnp.zeros(sums.shape, jnp.float32)

    def work(at, _):
        near = pl.ds(pl.multiple_of(at * LANES, LANES), LANES)
        cols = pl.ds(pl.multiple_of(first + at * LANES, LANES), LANES)
        for way in range(2):
            base = way * total
            places = [base + EDGE + (tap - REACH if way == 0 else REACH - tap) for tap in range(TAPS)]
            linear = values[base : base + total, near]
            logistic = jax.nn.sigmoid(linear)
            gating = linear * logistic
            halo = way * 2 * EDGE
            up = jnp.concatenate(
                [
                    ups_halo[halo : halo + EDGE, cols],
                    ups[way * rows : (way + 1) * rows, cols],
                    ups_halo[halo + EDGE : halo + 2 * EDGE, cols],
                ],
                axis=0,
            )
            grad_mix = up * gating
            mixes[way] = grad_mix
            mid = slice(EDGE, EDGE + rows)
            linear, logistic, gating, up, grad_mix = [
                cells[mid] for cells in (linear, logistic, gating, up, grad_mix)
            ]
            mixing = jnp.zeros((rows, LANES), jnp.float32)
            for tap in range(TAPS):
                moved = values[places[tap] : places[tap] + rows, near]
                mixing = mixing + taps[tap : tap + 1, cols] * moved
                sums[tap : tap + 1, near] += jnp.sum(grad_mix * moved, axis=0, keepdims=True)
            strand_out = mixing * gating
            acc = up * mixing * logistic * (1.0 + linear * (1.0 - logistic))
            for tap in range(TAPS):
                lower = 2 * EDGE - places[tap] + base
                acc = acc + taps[tap : tap + 1, cols] * mixes[way, lower : lower + rows]
            grads[way * rows : (way + 1) * rows, near] = acc.astype(jnp.bfloat16)
            if way == 0:
                ahead[:, near] = strand_out
            else:
                far = pl.ds(pl.multiple_of((count - 1 - at) * LANES, LANES), LANES)
                behind[:, far] = dot(strand_out.astype(jnp.bfloat16), turn)
        return 0

    lax.fori_loop(0, count, work, 0)


def product_kernel(columns, *refs, block, parts):
    grads, refs = refs[:parts], refs[parts:]
    out = refs[-1]
    start = 0
    for part in grads:
        stop = start + part.shape[1]
        out[:, start:stop] = dot(columns[block], part[...]).astype(out.dtype)
        start = stop
    if len(refs) > 1:
        out[:, start:] = refs[0][...]


def merge_kernel(columns, came, *refs, block, parts):
    grads, refs = refs[:parts], refs[parts:]
    out = refs[-1]
    start = 0
    for part in grads:
        stop = start + part.shape[1]
        own = dot(columns[block], part[...])
        out[:, start:stop] = (own + came[:, start:stop].astype(jnp.float32)).astype(jnp.bfloat16)
        start = stop
    if len(refs) > 1:
        out[:, start:] = paired(added(refs[0][...], came[:, start:])).astype(jnp.bfloat16)


def small_kernel(place, hot, w0, w1, w2, w3, *refs):
    parts, (out, grads, sums, table) = refs[:6], refs[6:]
    rows = hot.shape[1] // 3
    start = 0
    for at in range(3):
        part, part_sums = parts[at * 2], parts[at * 2 + 1]
        stop = start + part.shape[1]
        grads[:8, start:stop] = dot(hot[:, :rows], part[:rows])[:8]
        grads[8:, start:stop] = dot(hot[:, :rows], part[rows:])[:8]
        sums[:, start:stop] = part_sums[...]
        start = stop
    split = jnp.concatenate(thirds(grads[...]), axis=0)
    turn = turning(256)
    width = w0.shape[0]
    dims = (((1,), (1,)), ((), ()))
    backs = []
    for w in (w0, w1, w2, w3):
        back = lax.dot_general(split, w[...], dims, preferred_element_type=jnp.float32)
        backs.append(back[:16] + back[16:32] + back[32:])
    for r in range(4):
        cols = pl.ds(pl.multiple_of((place[0] ^ r) * width, width), width)
        there = turned(jnp.concatenate(thirds(backs[3 - r][8:]), axis=0), turn)
        table[:, cols] = backs[r][:8] + there[:8] + there[8:16] + there[16:]
    units = sums.shape[1]
    count = units // LANES
    for at in range(count):
        pack = jnp.concatenate(
            [
                sums[:, at * LANES : (at + 1) * LANES],
                table[:, at * LANES : (at + 1) * LANES],
                table[:, units + at * LANES : units + (at + 1) * LANES],
                jnp.zeros((8, LANES), jnp.float32),
            ],
            axis=0,
        )
        head = pack.astype(jnp.bfloat16).astype(jnp.float32)
        rest = pack - head
        low = low_lanes(pack.shape)
        first = jnp.where(low, head, pltpu.roll(rest, LANES // 2, 1))
        second = jnp.where(low, pltpu.roll(head, LANES // 2, 1), rest)
        out[at * PACK : (at + 1) * PACK] = first.astype(jnp.bfloat16)
        out[(count + at) * PACK : (count + at + 1) * PACK] = second.astype(jnp.bfloat16)


def back_kernel(place, w0, w1, w2, w3, later, *refs):
    parts, (out, block, backs, grads) = refs[:9], refs[9:]
    rows = out.shape[0]
    width = w0.shape[0]
    turn = turning(256)
    dims = (((1,), (1,)), ((), ()))
    start = 0
    for at in range(3):
        part = parts[at * 3]
        stop = start + part.shape[1]
        grads[:, start:stop] = part[...]
        start = stop
    forward = jnp.concatenate([parts[at * 3 + 1][...] for at in range(3)], axis=1)
    backward = jnp.concatenate([parts[at * 3 + 2][...] for at in (2, 1, 0)], axis=1)
    block[...] = (forward + backward).astype(jnp.bfloat16)
    for r, w in enumerate((w0, w1, w2, w3)):
        backs[r] = lax.dot_general(grads[...], w[...], dims, preferred_element_type=jnp.float32)
    for r in range(4):
        whole = backs[r, :rows] + turned(backs[3 - r, rows:].astype(jnp.bfloat16), turn)
        out[:, pl.ds(pl.multiple_of((place[0] ^ r) * width, width), width)] = whole.astype(jnp.bfloat16)


def block_kernel(place, columns, mate, came, *refs, parts):
    grads, refs = refs[:parts], refs[parts:]
    wide = len(refs) > 5
    if wide:
        merged, outs, own, extra = refs[0], refs[1:5], refs[5], refs[6]
        extra[...] = paired(added(merged[:, own.shape[1] :], came[:, own.shape[1] :]))
    else:
        outs, own = refs[:4], refs[4]
    rows = outs[0].shape[0]
    units = own.shape[1]
    product_kernel(columns, *grads, own, block=0, parts=parts)
    for step, out in enumerate(outs):
        here = pl.ds(pl.multiple_of((place[1] + step) % 4 * rows, rows), rows)
        out[:, :units] = added(own[here], mate[here], came[here, :units]).astype(jnp.bfloat16)
        if wide:
            out[:, units:] = extra[here].astype(jnp.bfloat16)


def quarter_kernel(*refs):
    head, tail, out = refs[:4], refs[4:8], refs[8]
    rows, units = head[0].shape
    size = 32

    def step(at, _):
        here = pl.ds(pl.multiple_of(at * size, size), size)
        out[here, :units] = added(*[part[here] for part in head]).astype(jnp.bfloat16)
        cells = added(*[part[here] for part in tail])
        out[here, units : 2 * units] = cells[:, :units].astype(jnp.bfloat16)
        out[here, 2 * units :] = paired(cells[:, units:]).astype(jnp.bfloat16)
        return 0

    lax.fori_loop(0, rows // size, step, 0)


def piece_kernel(parts, out):
    units = out.shape[2] - LANES
    total = parts[0].astype(jnp.float32)
    for at in range(1, parts.shape[0]):
        total = total + parts[at].astype(jnp.float32)
    plain = total[:, :units].astype(jnp.bfloat16)
    packed = paired(total[:, units:]).astype(jnp.bfloat16)
    for at in range(parts.shape[0]):
        out[at, :, :units] = plain
        out[at, :, units:] = packed


def final_kernel(place, q0, q1, q2, q3, weight_out, taps_out, table_out, packed, *, factor):
    rows = q0.shape[0]
    units = weight_out.shape[1]
    for step, part in enumerate((q0, q1, q2, q3)):
        there = pl.ds(pl.multiple_of((place[1] + 4 - step) % 4 * rows, rows), rows)
        weight_out[there] = part[:, :units].astype(jnp.float32) * factor
        packed[there] = part[:, units:].astype(jnp.float32)
    cells = packed[...]
    whole = cells + pltpu.roll(cells, LANES // 2, 1)
    half = whole.shape[0] // 2
    whole = jnp.where(low_lanes((half, LANES)), whole[:half], whole[half:]) * factor
    count = half // PACK
    symbols = table_out.shape[0]
    for at in range(count):
        cols = slice(at * LANES, (at + 1) * LANES)
        taps_out[:, cols] = whole[at * PACK : at * PACK + TAPS]
        table_out[:, cols] = whole[at * PACK + 8 : at * PACK + 8 + symbols]
        cols = slice(units + at * LANES, units + (at + 1) * LANES)
        table_out[:, cols] = whole[at * PACK + 16 : at * PACK + 16 + symbols]


def call(kernel, outs, *args, scratch=(), scalar=False, unread=(), **fixed):
    inside = pl.BlockSpec(memory_space=pltpu.VMEM)
    specs = [inside] * len(args)
    if scalar:
        specs[0] = pl.BlockSpec(memory_space=pltpu.SMEM)
    for at in unread:
        specs[at] = pl.BlockSpec(memory_space=pl.ANY)
    return pl.pallas_call(
        functools.partial(kernel, **fixed),
        out_shape=outs,
        in_specs=specs,
        out_specs=jax.tree.map(lambda _: inside, outs),
        scratch_shapes=list(scratch),
        compiler_params=pltpu.CompilerParams(vmem_limit_bytes=20 * 2**20),
    )(*args)


def array(shape, dtype=jnp.bfloat16):
    return jax.ShapeDtypeStruct(shape, dtype)


def step(hidden, tokens, embedding, weight, kernel, cotangent):
    window = hidden[0]
    upstream = cotangent[0]
    rows, features = window.shape
    units = weight.shape[1]
    symbols = embedding.shape[0]
    factor = 1.0 / math.sqrt(rows * 256)
    width = features // 4
    total = rows + 2 * EDGE
    me = 2 * lax.axis_index("xl") + lax.axis_index("c")
    place = jnp.stack([me, lax.axis_index("y")]).astype(jnp.int32)
    weights = [weight, swap_core(weight), side(weight)]
    weights.append(swap_core(weights[2]))
    top = pl.BlockSpec((EDGE, features), lambda at: (0, 0))
    bottom = pl.BlockSpec((EDGE, features), lambda at: (rows // EDGE - 1, 0))
    up_top = pl.BlockSpec((EDGE, units), lambda at: (0, 0))
    up_bottom = pl.BlockSpec((EDGE, units), lambda at: (rows // EDGE - 1, 0))
    edge = array((EDGE, features + units))
    before, after = pl.pallas_call(
        edge_kernel,
        out_shape=(edge, edge),
        grid=(1,),
        in_specs=[
            pl.BlockSpec(memory_space=pltpu.SMEM),
            bottom,
            top,
            up_bottom,
            up_top,
            pl.BlockSpec((symbols, features), lambda at: (0, 0)),
        ],
        out_specs=[pl.BlockSpec(edge.shape, lambda at: (0, 0))] * 2,
        scratch_shapes=[pltpu.VMEM((EDGE, features), jnp.float32)],
    )(tokens, window, window, upstream, upstream, embedding)
    before = shift(before, ("xh", "z", "y"), neighbour(1))
    after = shift(after, ("xh", "z", "y"), neighbour(-1))
    centre, columns, up_centre, taps, hot = call(
        centre_kernel,
        (
            array((4, 2 * rows, width)),
            array((4, width, 2 * rows)),
            array((2 * rows, units), jnp.float32),
            array(kernel.shape, jnp.float32),
            array((16, 3 * rows)),
        ),
        place,
        *[
            pltpu.with_memory_space_constraint(cells, pltpu.HBM)
            for cells in (tokens, kernel, window, embedding, upstream)
        ],
        scalar=True,
        unread=(1, 2, 3, 4, 5),
        scratch=(
            pltpu.VMEM((rows, features), jnp.bfloat16),
            pltpu.VMEM((symbols, features), jnp.float32),
            pltpu.VMEM((rows, units), jnp.bfloat16),
            pltpu.VMEM(tokens.shape, jnp.int32),
            pltpu.SemaphoreType.DMA((5,)),
        ),
    )
    partial = call(early_kernel, array((2 * rows, units), jnp.float32), centre, *weights[:2])
    halos, ups_halo, partial_halo = call(
        halo_kernel,
        (
            array((4, 4 * EDGE, width)),
            array((4 * EDGE, units), jnp.float32),
            array((4 * EDGE, units), jnp.float32),
        ),
        place,
        before,
        after,
        *weights[:2],
        scalar=True,
    )
    partial = call(
        middle_kernel,
        array((2 * total, units), jnp.float32),
        centre,
        halos,
        partial,
        partial_halo,
        weights[2],
        scratch=(pltpu.VMEM((2 * total, width), jnp.bfloat16),),
    )
    ends = (0, units // 2, units // 4 * 3, units)
    parts = []
    for at in range(3):
        size = ends[at + 1] - ends[at]
        parts.append(
            call(
                strand_kernel,
                (
                    array((2 * rows, size)),
                    array((rows, size), jnp.float32),
                    array((rows, size), jnp.float32),
                    array((8, size), jnp.float32),
                ),
                centre,
                halos,
                partial,
                weights[3],
                up_centre,
                ups_halo,
                taps,
                scratch=(
                    pltpu.VMEM((2 * total, size), jnp.float32),
                    pltpu.VMEM((2, total, LANES), jnp.float32),
                    pltpu.VMEM((2 * total, width), jnp.bfloat16),
                ),
                first=ends[at],
            )
        )
    grads = [[parts[0][0]], [parts[1][0], parts[2][0]]]
    extra = call(
        small_kernel,
        array((width, LANES)),
        place,
        hot,
        *weights,
        *[cells for part in parts for cells in (part[0], part[3])],
        scalar=True,
        scratch=(
            pltpu.VMEM((16, units), jnp.float32),
            pltpu.VMEM((8, units), jnp.float32),
            pltpu.VMEM((8, features), jnp.float32),
        ),
    )
    chunk = array((width, units // 2))
    came = []
    mates = []
    for at in range(2):
        count = len(grads[at])
        rest = [extra] * at
        large = array((width, units // 2 + LANES * at))
        goes = call(product_kernel, large, columns, *grads[at], *rest, block=3, parts=count)
        goes = swap_core(goes)
        merged = call(merge_kernel, large, columns, goes, *grads[at], *rest, block=2, parts=count)
        came.append(side(merged))
        mate = call(product_kernel, chunk, columns, *grads[at], block=1, parts=count)
        mates.append(swap_core(mate))
    part = width // 4
    own = pltpu.VMEM(chunk.shape, jnp.float32)
    head = call(
        block_kernel,
        (array((part, units // 2)),) * 4,
        place,
        columns,
        mates[0],
        came[0],
        *grads[0],
        scalar=True,
        scratch=(own,),
        parts=1,
    )
    head = [head[0]] + [along_y(head[step], step) for step in (1, 2, 3)]
    tail = call(
        block_kernel,
        (array((part, units // 2 + LANES)),) * 4,
        place,
        columns,
        mates[1],
        came[1],
        *grads[1],
        merged,
        scalar=True,
        scratch=(own, pltpu.VMEM((width, LANES), jnp.float32)),
        parts=2,
    )
    grad_hidden, block_result = call(
        back_kernel,
        (array((rows, features)), array((rows, units))),
        place,
        *weights,
        tail[0],
        *[cells for part in parts for cells in part[:3]],
        scalar=True,
        unread=(5,),
        scratch=(pltpu.VMEM((4, 2 * rows, width), jnp.float32), pltpu.VMEM((2 * rows, units), jnp.bfloat16)),
    )
    tail = [tail[0]] + [along_y(tail[step], step) for step in (1, 2, 3)]
    quarter = call(quarter_kernel, array((part, units + LANES)), *head, *tail)
    pieces = quarter.reshape(16, part // 16, -1)
    pieces = lax.all_to_all(pieces, ("xh", "z"), split_axis=0, concat_axis=0, tiled=True)
    pieces = call(piece_kernel, array(pieces.shape), pieces)
    pieces = lax.all_to_all(pieces, ("xh", "z"), split_axis=0, concat_axis=0, tiled=True)
    quarter = pieces.reshape(quarter.shape)
    quarters = [quarter] + [along_y(quarter, step) for step in (1, 2, 3)]
    grad_weight, grad_kernel, grad_embedding = call(
        final_kernel,
        (array((width, units), jnp.float32), array(kernel.shape, jnp.float32), array(embedding.shape, jnp.float32)),
        place,
        *quarters,
        scalar=True,
        scratch=(pltpu.VMEM((width, LANES), jnp.float32),),
        factor=factor,
    )
    return block_result[None], grad_hidden[None], grad_weight, grad_kernel, grad_embedding


def solution(mesh):
    fine = Mesh(mesh.devices.reshape(SIZES), AXES)
    batch = ("xl", "c")
    spot = ("xh", "z", "y")
    in_specs = (P(batch, spot, None), P(batch, spot), P(), P(batch, None), P(), P(batch, spot, None))
    out_specs = (P(batch, spot, None), P(batch, spot, None), P(batch, None), P(), P())
    return jax.shard_map(step, mesh=fine, in_specs=in_specs, out_specs=out_specs, check_vma=False)
```
